512 devices in a mesh: side: 2 (over core), grp: 16 (over y, x), ex: 16 (over z).
Axes of the slice: x: 4, y: 4, z: 16, core: 2. Of those that a mesh axis runs over, the one named last changes fastest.
Arguments:
- tokens: bfloat16 [768, 7168], P(('grp', 'ex'), 'side'), may hold values from -6 to 6
- expert_ids: int32 [768, 8], P(('grp', 'ex')), may hold values from 0 to 15, all different within a row; in each aligned block of 3 rows (0 to 2, 3 to 5, ...) at most 3 rows name the same one
- scores: float32 [768, 8], P(('grp', 'ex')), may hold values from -8 to 8
- gate_weight: bfloat16 [16, 7168, 2048], P('ex', 'side', 'grp'), may hold values from -0.0625 to 0.0625
- up_weight: bfloat16 [16, 7168, 2048], P('ex', 'side', 'grp'), may hold values from -0.0625 to 0.0625
- down_weight: bfloat16 [16, 2048, 7168], P('ex', None, ('side', 'grp')), may hold values from -0.125 to 0.125
Outputs:
- combined: bfloat16 [768, 7168], P(('grp', 'ex'), 'side')
The draws below stay inside these ranges and needn't reach their ends.
Inputs may be any that keep to these rules, and one draw needn't show every extreme that they name: `expert_ids`: each row names 8 different experts; every expert is named by some row.
All inputs are finite; a program needn't handle non-finite values.
Results may differ from the reference program's by a relative error of at most 0.011.
Values may be sent and summed in bfloat16 or wider, within the bound.
No kernel may reach another device: no remote copies, remote signals or barrier semaphores. Data moves between devices by JAX's collectives and lax.ppermute only.
A program may use at most 64 MiB of HBM per device.

```python
import math
import jax
import jax.numpy as jnp
import numpy as np
from jax import lax

D = 7168
H = 2048
TOP = 8
EXPERTS = 16
TOK_DEV = 3
TOKENS = 768


def shard_levels(own_key, extent, split, smallest, largest):
    gain, own = 1.0, jax.random.fold_in(own_key, 6)
    for dim, parts in split:
        draws = jnp.exp(jax.random.uniform(jax.random.fold_in(own, dim), (parts,), jnp.float32, smallest / len(split), largest / len(split)))
        gain = gain * jnp.repeat(draws, extent[dim] // parts).reshape([-1 if axis == dim else 1 for axis in range(len(extent))])
    return gain


def assign_block(stream_key, own, number, rows, amount, top, bound, skew):
    ranking = jax.random.permutation(stream_key, amount)
    heavy_load, usual = portions_of(amount, rows * top, bound, skew, True), portions_of(amount, rows * top, bound, skew, False)
    places = jnp.arange(amount)

    def named(lengths, turn):
        used = int((lengths > 0).sum())
        fixed = max(1, used // 4)
        moved = fixed + (places - fixed + turn * (used - fixed)) % max(1, amount - fixed)
        return jnp.zeros((amount,), jnp.int32).at[ranking[jnp.where(places < fixed, places, moved)]].set(jnp.asarray(lengths, jnp.int32))

    lengths = jnp.where(number % 4 == 0, named(heavy_load, number // 4), named(usual, number - number // 4 - 1))
    mixed = jax.random.permutation(jax.random.fold_in(own, 3), amount)
    giver, taker = mixed[0:amount // 2 * 2:2], mixed[1:amount // 2 * 2:2]
    room = jnp.minimum(lengths[giver] - 1, bound - lengths[taker]) // 2
    room = jnp.where((giver == ranking[0]) | (taker == ranking[0]) | (lengths[taker] == 0), 0, jnp.maximum(room, 0))
    moved = jax.random.randint(jax.random.fold_in(own, 4), (amount // 2,), 0, 1 << 20) % (room + 1)
    lengths = lengths.at[giver].add(-moved).at[taker].add(moved)
    items = jnp.searchsorted(jnp.cumsum(lengths), jnp.arange(rows * top), side="right").astype(jnp.int32)
    table = items.reshape(top, rows).T
    table = table[jax.random.permutation(jax.random.fold_in(own, 1), rows)]
    turn = jax.random.randint(jax.random.fold_in(own, 2), (rows, 1), 0, top)
    return jnp.take_along_axis(table, (jnp.arange(top)[None, :] + turn) % top, axis=1)


def portions_of(amount, total, bound, slope, full):
    loads = [(1 << 20) // math.isqrt(grade ** slope) + 1 for grade in range(1, amount + 1)]
    largest = bound if full else min(bound, max(-(-total // amount), total * loads[0] // sum(loads)))
    least = 1 if total - largest >= amount - 1 else 0
    given, rest = [largest] + [least] * (amount - 1), total - largest - least * (amount - 1)
    while rest > 0:
        movable = [i for i in range(1, amount) if given[i] < largest] or [i for i in range(1, amount) if given[i] < bound]
        whole, left = sum([loads[i] for i in movable]), rest
        for i in movable:
            addition = min(bound - given[i], max(1, left * loads[i] // whole), rest)
            given[i] = given[i] + addition
            rest = rest - addition
    return np.array(given)


def centred(stream_key, extent, scale, reach, split=(), dtype=jnp.bfloat16):
    array = scale * jax.random.normal(stream_key, extent, jnp.float32)
    if split:
        array = array * shard_levels(stream_key, extent, split, -0.22, 0.18)
    return jnp.clip(array, -reach, reach).astype(dtype)


def setup_inputs(seed: int = 0) -> dict:
    key_list = jax.random.split(jax.random.key(seed), 7)
    tokens = centred(key_list[0], (TOKENS, D), 1.0, 6.0, ((0, 256), (1, 2)))
    expert_ids_keys = jax.random.split(jax.random.fold_in(key_list[1], 1), TOKENS // TOK_DEV)
    expert_ids_turns = jax.random.permutation(jax.random.fold_in(key_list[1], 3), TOKENS // TOK_DEV)
    expert_ids = jax.vmap(lambda own, number: assign_block(jax.random.fold_in(key_list[1], 2), own, number, TOK_DEV, EXPERTS, TOP, TOK_DEV, 2))(expert_ids_keys, expert_ids_turns).reshape((TOKENS, TOP))
    scores = centred(key_list[2], (TOKENS, TOP), 2.0, 8.0, ((0, 256),), jnp.float32)
    gate_weight = centred(key_list[3], (EXPERTS, D, H), D ** -0.5, 0.0625, ((0, 16), (1, 2), (2, 16)))
    up_weight = centred(key_list[4], (EXPERTS, D, H), D ** -0.5, 0.0625, ((0, 16), (1, 2), (2, 16)))
    down_weight = centred(key_list[5], (EXPERTS, H, D), H ** -0.5, 0.125, ((0, 16), (2, 32)))
    return {"tokens": tokens, "expert_ids": expert_ids, "scores": scores, "gate_weight": gate_weight, "up_weight": up_weight, "down_weight": down_weight}


def reference(tokens, expert_ids, scores, gate_weight, up_weight, down_weight):
    lifted = jax.nn.sigmoid(scores)
    route_weight = 2.5 * lifted / jnp.sum(lifted, axis=-1, keepdims=True)

    def add_expert(expert, total):
        gate_cols = lax.dynamic_index_in_dim(gate_weight, expert, 0, keepdims=False)
        up_cols = lax.dynamic_index_in_dim(up_weight, expert, 0, keepdims=False)
        down_rows = lax.dynamic_index_in_dim(down_weight, expert, 0, keepdims=False)
        gate = jnp.dot(tokens, gate_cols, preferred_element_type=jnp.float32)
        up_part = jnp.dot(tokens, up_cols, preferred_element_type=jnp.float32)
        hidden = (jax.nn.silu(gate) * up_part).astype(jnp.bfloat16)
        output = jnp.dot(hidden, down_rows, preferred_element_type=jnp.float32).astype(jnp.bfloat16)
        factor = jnp.sum(jnp.where(expert_ids == expert, route_weight, 0.0), axis=-1)
        return total + factor[:, None] * output.astype(jnp.float32)

    total = lax.fori_loop(0, EXPERTS, add_expert, jnp.zeros(tokens.shape, jnp.float32))
    return total.astype(jnp.bfloat16)
```

```python
import jax
import jax.numpy as jnp
from jax import lax
from jax.sharding import PartitionSpec as P


def dot(a, b, ca, cb):
    return lax.dot_general(
        a, b, (((ca,), (cb,)), ((), ())), preferred_element_type=jnp.float32
    )


def spread(block, axis):
    n = lax.axis_size(axis)
    copies = jnp.broadcast_to(block[None], (n, *block.shape))
    return lax.all_to_all(copies, axis, split_axis=0, concat_axis=0, tiled=True)


def per_device(tokens, expert_ids, scores, gate_weight, up_weight, down_weight):
    groups = lax.axis_size("grp")
    owners = lax.axis_size("ex")
    side = lax.axis_index("side")
    own, half_width = tokens.shape
    local_hidden = gate_weight.shape[2]
    share = local_hidden // 2
    hidden_total, out_width = down_weight.shape[1:]
    rows = own * owners
    total = rows * groups
    swap = [(0, 1), (1, 0)]

    lifted = jax.nn.sigmoid(scores)
    route_weight = 2.5 * lifted / jnp.sum(lifted, axis=-1, keepdims=True)
    named = expert_ids[:, :, None] == jnp.arange(owners, dtype=jnp.int32)
    table = jnp.sum(jnp.where(named, route_weight[:, :, None], 0.0), axis=1)

    gate, up = gate_weight[0], up_weight[0]
    low = jnp.concatenate([gate[:, :share], up[:, :share]], axis=1)
    high = jnp.concatenate([gate[:, share:], up[:, share:]], axis=1)
    first = side == 0
    kept = jnp.where(first, low, high)
    given = jnp.where(first, high, low)
    down = down_weight[0].reshape(groups, 2, share, out_width)
    down_low = down[:, 0].reshape(groups * share, out_width)
    down_high = down[:, 1].reshape(groups * share, out_width)
    down_kept = jnp.where(first, down_low, down_high)
    down_given = jnp.where(first, down_high, down_low)

    column = spread(tokens, "ex").reshape(rows, half_width)
    everyone = lax.all_gather(column, "grp", axis=0, tiled=True)

    outgoing = dot(given, everyone, 0, 1).astype(jnp.bfloat16)
    arrived = lax.ppermute(outgoing, "side", swap)
    summed = dot(kept, everyone, 0, 1) + arrived.astype(jnp.float32)
    hidden = (jax.nn.silu(summed[:share]) * summed[share:]).astype(jnp.bfloat16)

    mine = spread(hidden, "grp").reshape(groups * share, total)
    other = lax.ppermute(mine, "side", swap)
    expert_out = dot(mine, down_kept, 0, 0) + dot(other, down_given, 0, 0)
    expert_out = expert_out.astype(jnp.bfloat16)

    by_group = lax.all_to_all(
        expert_out.reshape(groups, rows, out_width), "grp", split_axis=0, concat_axis=0, tiled=True
    ).reshape(total, out_width)
    place = jnp.arange(total, dtype=jnp.int32)
    source = (place // own) % groups * rows + place // (groups * own) * own + place % own
    permute = (source[:, None] == place[None, :]).astype(jnp.bfloat16)
    turned = dot(permute, by_group, 1, 0).astype(jnp.bfloat16)
    back = lax.all_to_all(
        turned.reshape(owners, groups * own, out_width), "ex", split_axis=0, concat_axis=0, tiled=True
    )
    factor = jnp.tile(table, (groups, 1)).T[:, :, None]
    combined = jnp.sum(back.astype(jnp.float32) * factor, axis=0).astype(jnp.bfloat16)
    combined = combined.reshape(groups, own, out_width)
    return jnp.transpose(combined, (1, 0, 2)).reshape(own, half_width)


def solution(mesh):
    in_specs = (
        P(("grp", "ex"), "side"),
        P(("grp", "ex"), None),
        P(("grp", "ex"), None),
        P("ex", "side", "grp"),
        P("ex", "side", "grp"),
        P("ex", None, ("side", "grp")),
    )
    out_specs = P(("grp", "ex"), "side")
    return jax.shard_map(
        per_device, mesh=mesh, in_specs=in_specs, out_specs=out_specs, check_vma=False
    )
```

```python
import jax
import jax.numpy as jnp
from jax import lax
from jax.experimental import pallas as pl
from jax.experimental.pallas import tpu as pltpu
from jax.sharding import Mesh
from jax.sharding import PartitionSpec as P

GRP = ("y", "x")
SWAP = [(0, 1), (1, 0)]


def dot(a, b, ca, cb):
    return lax.dot_general(
        a, b, (((ca,), (cb,)), ((), ())), preferred_element_type=jnp.float32
    )


def exchange(blocks, axis):
    return lax.all_to_all(blocks, axis, split_axis=0, concat_axis=0, tiled=True)


def copies(block, n):
    return jnp.broadcast_to(block[None], (n, *block.shape))


def gate_up_kernel(place, tokens, piece0, piece1, piece2, piece3, kept, given):
    share = kept.shape[1] // 2
    for step, piece in enumerate((piece0, piece1, piece2, piece3)):
        weight = jnp.concatenate([piece[0], piece[1]], axis=1)
        sums = dot(weight, tokens[...], 0, 1)
        owner = place[0] ^ step
        for side in range(2):
            low, high = side * share, (1 - side) * share

            @pl.when(place[1] == side)
            def _():
                kept[owner] = jnp.concatenate(
                    [sums[low : low + share], sums[2 * share + low : 3 * share + low]], axis=0
                )
                given[owner] = jnp.concatenate(
                    [sums[high : high + share], sums[2 * share + high : 3 * share + high]], axis=0
                ).astype(given.dtype)


def gate_up(place, tokens, pieces):
    units, total = pieces[0].shape[2], tokens.shape[0]
    shape = (len(pieces), units, total)
    vmem = pl.BlockSpec(memory_space=pltpu.VMEM)
    return pl.pallas_call(
        gate_up_kernel,
        out_shape=(
            jax.ShapeDtypeStruct(shape, jnp.float32),
            jax.ShapeDtypeStruct(shape, jnp.bfloat16),
        ),
        in_specs=[pl.BlockSpec(memory_space=pltpu.SMEM)] + [vmem] * 5,
        out_specs=(vmem, vmem),
        compiler_params=pltpu.CompilerParams(vmem_limit_bytes=32 * 2**20),
    )(place, tokens, *pieces)


def per_device(tokens, expert_ids, scores, gate_weight, up_weight, down_weight):
    across = lax.axis_size("x")
    groups = lax.axis_size("y") * across
    owners = lax.axis_size("ex")
    side, col = lax.axis_index("side"), lax.axis_index("x")
    own, half_width = tokens.shape
    share = gate_weight.shape[2] // 2
    out_width = down_weight.shape[2]
    rows = own * owners
    total = rows * groups
    part = half_width // across

    lifted = jax.nn.sigmoid(scores)
    route_weight = 2.5 * lifted / jnp.sum(lifted, axis=-1, keepdims=True)
    named = expert_ids[:, :, None] == jnp.arange(owners, dtype=jnp.int32)
    table = jnp.sum(jnp.where(named, route_weight[:, :, None], 0.0), axis=1)
    factor = jnp.tile(table, (groups, 1)).T[:, :, None]
    index = jnp.arange(total, dtype=jnp.int32)
    source = (index // own) % groups * rows + index // (groups * own) * own + index % own

    def rows_of(step):
        start = (col ^ step) * part
        return jnp.stack(
            [lax.dynamic_slice_in_dim(w[0], start, part, 0) for w in (gate_weight, up_weight)]
        )

    pieces = [rows_of(0)] + [
        lax.ppermute(rows_of(d), "x", [(i, i ^ d) for i in range(across)]) for d in range(1, across)
    ]

    column = exchange(copies(tokens.reshape(-1, 4, 128), owners), "ex").reshape(rows, half_width)
    parts = jnp.transpose(column.reshape(rows, across, part), (1, 0, 2))
    parts, pieces, factor, source = lax.optimization_barrier((parts, pieces, factor, source))
    everyone = exchange(copies(parts, groups // across).reshape(groups, rows, part), GRP)
    everyone = everyone.reshape(total, part)

    place = jnp.stack([col, side]).astype(jnp.int32)
    kept, given = gate_up(place, everyone, pieces)
    arrived = lax.ppermute(given, "side", SWAP)
    blocks = (kept + arrived.astype(jnp.float32)).astype(jnp.bfloat16)
    summed = jnp.sum(exchange(blocks, "x").astype(jnp.float32), axis=0)
    hidden = (jax.nn.silu(summed[:share]) * summed[share:]).astype(jnp.bfloat16)

    down = down_weight[0].reshape(groups, 2, share, out_width)
    down_low = down[:, 0].reshape(groups * share, out_width)
    down_high = down[:, 1].reshape(groups * share, out_width)
    down_kept = jnp.where(side == 0, down_low, down_high)
    down_given = jnp.where(side == 0, down_high, down_low)
    mine = exchange(copies(hidden, groups), GRP).reshape(groups * share, total)
    other = lax.ppermute(mine, "side", SWAP)
    expert_out = dot(mine, down_kept, 0, 0) + dot(other, down_given, 0, 0)
    expert_out = expert_out.astype(jnp.bfloat16)

    by_group = exchange(expert_out.reshape(groups, rows, out_width), GRP).reshape(total, out_width)
    permute = (source[:, None] == index[None, :]).astype(jnp.bfloat16)
    turned = dot(permute, by_group, 1, 0).astype(jnp.bfloat16)
    back = exchange(turned.reshape(owners, groups * own, out_width), "ex")

    combined = jnp.sum(back.astype(jnp.float32) * factor, axis=0).astype(jnp.bfloat16)
    combined = combined.reshape(groups, own, out_width)
    return jnp.transpose(combined, (1, 0, 2)).reshape(own, half_width)


def solution(mesh):
    sides, groups, owners = mesh.devices.shape
    fine = Mesh(mesh.devices.reshape(sides, groups // 4, 4, owners), ("side", "y", "x", "ex"))
    in_specs = (
        P(("y", "x", "ex"), "side"),
        P(("y", "x", "ex"), None),
        P(("y", "x", "ex"), None),
        P("ex", "side", GRP),
        P("ex", "side", GRP),
        P("ex", None, ("side", "y", "x")),
    )
    out_specs = P(("y", "x", "ex"), "side")
    return jax.shard_map(
        per_device, mesh=fine, in_specs=in_specs, out_specs=out_specs, check_vma=False
    )
```

```python
import jax
import jax.numpy as jnp
from jax import lax
from jax.experimental import pallas as pl
from jax.experimental.pallas import tpu as pltpu
from jax.sharding import Mesh
from jax.sharding import PartitionSpec as P

GRP = ("yh", "yl", "xh", "xl")
BLOCK = ("yl", "xl")
SWAP = [(0, 1), (1, 0)]


def dot(a, b, ca, cb):
    return lax.dot_general(
        a, b, (((ca,), (cb,)), ((), ())), preferred_element_type=jnp.float32
    )


def exchange(blocks, axis):
    return lax.all_to_all(blocks, axis, split_axis=0, concat_axis=0, tiled=True)


def copies(block, n):
    return jnp.broadcast_to(block[None], (n, *block.shape))


def swap_in_block(x, step):
    return lax.ppermute(x, BLOCK, [(i, i ^ step) for i in range(4)])


def gate_up_kernel(which, tokens, piece0, piece1, piece2, piece3, kept, given):
    share = kept.shape[1] // 2
    for step, piece in enumerate((piece0, piece1, piece2, piece3)):
        weight = jnp.concatenate([piece[0], piece[1]], axis=1)
        sums = dot(weight, tokens[...], 0, 1)
        for side in range(2):
            low, high = side * share, (1 - side) * share

            @pl.when(which[0] == side)
            def _():
                kept[step] = jnp.concatenate(
                    [sums[low : low + share], sums[2 * share + low : 3 * share + low]], axis=0
                )
                given[step] = jnp.concatenate(
                    [sums[high : high + share], sums[2 * share + high : 3 * share + high]], axis=0
                ).astype(given.dtype)


def gate_up(side, tokens, pieces):
    units, total = pieces[0].shape[2], tokens.shape[0]
    shape = (len(pieces), units, total)
    vmem = pl.BlockSpec(memory_space=pltpu.VMEM)
    return pl.pallas_call(
        gate_up_kernel,
        out_shape=(
            jax.ShapeDtypeStruct(shape, jnp.float32),
            jax.ShapeDtypeStruct(shape, jnp.bfloat16),
        ),
        in_specs=[pl.BlockSpec(memory_space=pltpu.SMEM)] + [vmem] * 5,
        out_specs=(vmem, vmem),
        compiler_params=pltpu.CompilerParams(vmem_limit_bytes=32 * 2**20),
    )(side, tokens, *pieces)


def per_device(tokens, expert_ids, scores, gate_weight, up_weight, down_weight):
    across = lax.axis_size(BLOCK)
    groups = lax.axis_size(GRP)
    owners = lax.axis_size("ex")
    side, col = lax.axis_index("side"), lax.axis_index(BLOCK)
    own, half_width = tokens.shape
    share = gate_weight.shape[2] // 2
    out_width = down_weight.shape[2]
    rows = own * owners
    total = rows * groups
    part = half_width // across

    lifted = jax.nn.sigmoid(scores)
    route_weight = 2.5 * lifted / jnp.sum(lifted, axis=-1, keepdims=True)
    named = expert_ids[:, :, None] == jnp.arange(owners, dtype=jnp.int32)
    table = jnp.sum(jnp.where(named, route_weight[:, :, None], 0.0), axis=1)
    factor = jnp.tile(table, (groups, 1)).T[:, :, None]
    index = jnp.arange(total, dtype=jnp.int32)
    source = (index // own) % groups * rows + index // (groups * own) * own + index % own

    def rows_of(step):
        start = (col ^ step) * part
        return jnp.stack(
            [lax.dynamic_slice_in_dim(w[0], start, part, 0) for w in (gate_weight, up_weight)]
        )

    pieces = [rows_of(0)] + [swap_in_block(rows_of(d), d) for d in range(1, across)]

    column = exchange(copies(tokens.reshape(-1, 4, 128), owners), "ex").reshape(rows, half_width)
    parts = jnp.transpose(column.reshape(rows, across, part), (1, 0, 2))
    parts, pieces, factor, source = lax.optimization_barrier((parts, pieces, factor, source))
    fan = jnp.broadcast_to(
        parts.reshape(1, 2, 1, 2, rows, part), (2, 2, 2, 2, rows, part)
    ).reshape(groups, rows, part)
    everyone = exchange(fan, GRP).reshape(total, part)

    kept, given = gate_up(side.reshape(1), everyone, pieces)
    arrived = lax.ppermute(given, "side", SWAP)
    sums = [kept[d] + arrived[d].astype(jnp.float32) for d in range(across)]
    summed = sums[0]
    for d in (3, 1, 2):
        summed = summed + swap_in_block(sums[d].astype(jnp.bfloat16), d).astype(jnp.float32)
    hidden = (jax.nn.silu(summed[:share]) * summed[share:]).astype(jnp.bfloat16)

    down = down_weight[0].reshape(groups, 2, share, out_width)
    down_low = down[:, 0].reshape(groups * share, out_width)
    down_high = down[:, 1].reshape(groups * share, out_width)
    down_kept = jnp.where(side == 0, down_low, down_high)
    down_given = jnp.where(side == 0, down_high, down_low)
    mine = exchange(copies(hidden, groups), GRP).reshape(groups * share, total)
    other = lax.ppermute(mine, "side", SWAP)
    expert_out = dot(mine, down_kept, 0, 0) + dot(other, down_given, 0, 0)
    expert_out = expert_out.astype(jnp.bfloat16)

    by_group = exchange(expert_out.reshape(groups, rows, out_width), GRP).reshape(total, out_width)
    permute = (source[:, None] == jnp.arange(total, dtype=jnp.int32)).astype(jnp.bfloat16)
    turned = dot(permute, by_group, 1, 0).astype(jnp.bfloat16)
    back = exchange(turned.reshape(owners, groups * own, out_width), "ex")
    combined = jnp.sum(back.astype(jnp.float32) * factor, axis=0).astype(jnp.bfloat16)
    combined = combined.reshape(groups, own, out_width)
    return jnp.transpose(combined, (1, 0, 2)).reshape(own, half_width)


def solution(mesh):
    sides, groups, owners = mesh.devices.shape
    names = ("side", *GRP, "ex")
    fine = Mesh(mesh.devices.reshape(sides, 2, 2, 2, groups // 8, owners), names)
    in_specs = (
        P((*GRP, "ex"), "side"),
        P((*GRP, "ex"), None),
        P((*GRP, "ex"), None),
        P("ex", "side", GRP),
        P("ex", "side", GRP),
        P("ex", None, ("side", *GRP)),
    )
    out_specs = P((*GRP, "ex"), "side")
    return jax.shard_map(
        per_device, mesh=fine, in_specs=in_specs, out_specs=out_specs, check_vma=False
    )
```

```python
import jax
import jax.numpy as jnp
from jax import lax
from jax.experimental import pallas as pl
from jax.experimental.pallas import tpu as pltpu
from jax.sharding import Mesh
from jax.sharding import PartitionSpec as P

GRP = ("yh", "yl", "xh", "xl")
BLOCK = ("yl", "xl")
SWAP = [(0, 1), (1, 0)]


def dot(a, b, ca, cb):
    return lax.dot_general(
        a, b, (((ca,), (cb,)), ((), ())), preferred_element_type=jnp.float32
    )


def exchange(blocks, axis):
    return lax.all_to_all(blocks, axis, split_axis=0, concat_axis=0, tiled=True)


def copies(block, n):
    return jnp.broadcast_to(block[None], (n, *block.shape))


def swap_in_block(x, step):
    return lax.ppermute(x, BLOCK, [(i, i ^ step) for i in range(4)])


def gate_up_kernel(which, tokens, piece0, piece1, piece2, piece3, kept, given):
    share = kept.shape[1] // 2
    for step, piece in enumerate((piece0, piece1, piece2, piece3)):
        weight = jnp.concatenate([piece[0], piece[1]], axis=1)
        sums = dot(weight, tokens[...], 0, 1)
        for side in range(2):
            low, high = side * share, (1 - side) * share

            @pl.when(which[0] == side)
            def _():
                kept[step] = jnp.concatenate(
                    [sums[low : low + share], sums[2 * share + low : 3 * share + low]], axis=0
                )
                given[step] = jnp.concatenate(
                    [sums[high : high + share], sums[2 * share + high : 3 * share + high]], axis=0
                ).astype(given.dtype)


def gate_up(side, tokens, pieces):
    units, total = pieces[0].shape[2], tokens.shape[0]
    shape = (len(pieces), units, total)
    vmem = pl.BlockSpec(memory_space=pltpu.VMEM)
    return pl.pallas_call(
        gate_up_kernel,
        out_shape=(
            jax.ShapeDtypeStruct(shape, jnp.float32),
            jax.ShapeDtypeStruct(shape, jnp.bfloat16),
        ),
        in_specs=[pl.BlockSpec(memory_space=pltpu.SMEM)] + [vmem] * 5,
        out_specs=(vmem, vmem),
        compiler_params=pltpu.CompilerParams(vmem_limit_bytes=32 * 2**20),
    )(side, tokens, *pieces)


def combine_kernel(back, table, out):
    owners, rows, width = back.shape
    own = table.shape[0]
    groups = rows // own
    weight = jnp.concatenate([table[...]] * groups, axis=0)
    total = back[0].astype(jnp.float32) * weight[:, :1]
    for owner in range(1, owners):
        total = total + back[owner].astype(jnp.float32) * weight[:, owner : owner + 1]
    wide = jnp.concatenate([total[g * own : (g + 1) * own] for g in range(groups)], axis=1)
    out[...] = wide.astype(out.dtype)


def combine(back, table):
    owners, rows, width = back.shape
    own = table.shape[0]
    vmem = pl.BlockSpec(memory_space=pltpu.VMEM)
    return pl.pallas_call(
        combine_kernel,
        out_shape=jax.ShapeDtypeStruct((own, rows // own * width), jnp.bfloat16),
        in_specs=[vmem, vmem],
        out_specs=vmem,
        compiler_params=pltpu.CompilerParams(vmem_limit_bytes=16 * 2**20),
    )(back, table)


def per_device(tokens, expert_ids, scores, gate_weight, up_weight, down_weight):
    across = lax.axis_size(BLOCK)
    groups = lax.axis_size(GRP)
    owners = lax.axis_size("ex")
    side, col = lax.axis_index("side"), lax.axis_index(BLOCK)
    own, half_width = tokens.shape
    share = gate_weight.shape[2] // 2
    out_width = down_weight.shape[2]
    rows = own * owners
    total = rows * groups
    part = half_width // across

    lifted = jax.nn.sigmoid(scores)
    route_weight = 2.5 * lifted / jnp.sum(lifted, axis=-1, keepdims=True)
    named = expert_ids[:, :, None] == jnp.arange(owners, dtype=jnp.int32)
    table = jnp.sum(jnp.where(named, route_weight[:, :, None], 0.0), axis=1)
    index = jnp.arange(total, dtype=jnp.int32)
    source = (index // own) % groups * rows + index // (groups * own) * own + index % own

    def rows_of(step):
        start = (col ^ step) * part
        return jnp.stack(
            [lax.dynamic_slice_in_dim(w[0], start, part, 0) for w in (gate_weight, up_weight)]
        )

    pieces = [rows_of(0)] + [swap_in_block(rows_of(d), d) for d in range(1, across)]

    column = exchange(copies(tokens.reshape(-1, 4, 128), owners), "ex").reshape(rows, half_width)
    parts = jnp.transpose(column.reshape(rows, across, part), (1, 0, 2))
    parts, pieces, table, source = lax.optimization_barrier((parts, pieces, table, source))
    fan = jnp.broadcast_to(
        parts.reshape(1, 2, 1, 2, rows, part), (2, 2, 2, 2, rows, part)
    ).reshape(groups, rows, part)
    everyone = exchange(fan, GRP).reshape(total, part)

    kept, given = gate_up(side.reshape(1), everyone, pieces)
    arrived = lax.ppermute(given, "side", SWAP)
    sums = [kept[d] + arrived[d].astype(jnp.float32) for d in range(across)]
    summed = sums[0]
    for d in (3, 1, 2):
        summed = summed + swap_in_block(sums[d].astype(jnp.bfloat16), d).astype(jnp.float32)
    hidden = (jax.nn.silu(summed[:share]) * summed[share:]).astype(jnp.bfloat16)

    down = down_weight[0].reshape(groups, 2, share, out_width)
    down_low = down[:, 0].reshape(groups * share, out_width)
    down_high = down[:, 1].reshape(groups * share, out_width)
    down_kept = jnp.where(side == 0, down_low, down_high)
    down_given = jnp.where(side == 0, down_high, down_low)
    mine = exchange(copies(hidden, groups), GRP).reshape(groups * share, total)
    other = lax.ppermute(mine, "side", SWAP)
    expert_out = dot(mine, down_kept, 0, 0) + dot(other, down_given, 0, 0)
    expert_out = expert_out.astype(jnp.bfloat16)

    by_group = exchange(expert_out.reshape(groups, rows, out_width), GRP).reshape(total, out_width)
    permute = (source[:, None] == jnp.arange(total, dtype=jnp.int32)).astype(jnp.bfloat16)
    turned = dot(permute, by_group, 1, 0).astype(jnp.bfloat16)
    turned, table = lax.optimization_barrier((turned, table))
    back = exchange(turned.reshape(owners, groups * own, out_width), "ex")
    return combine(back, table)


def solution(mesh):
    sides, groups, owners = mesh.devices.shape
    names = ("side", *GRP, "ex")
    fine = Mesh(mesh.devices.reshape(sides, 2, 2, 2, groups // 8, owners), names)
    in_specs = (
        P((*GRP, "ex"), "side"),
        P((*GRP, "ex"), None),
        P((*GRP, "ex"), None),
        P("ex", "side", GRP),
        P("ex", "side", GRP),
        P("ex", None, ("side", *GRP)),
    )
    out_specs = P((*GRP, "ex"), "side")
    return jax.shard_map(
        per_device, mesh=fine, in_specs=in_specs, out_specs=out_specs, check_vma=False
    )
```

```python
import jax
import jax.numpy as jnp
from jax import lax
from jax.experimental import pallas as pl
from jax.experimental.pallas import tpu as pltpu
from jax.sharding import Mesh
from jax.sharding import PartitionSpec as P

GRP = ("yh", "yl", "xh", "xl")
BLOCK = ("yl", "xl")
SWAP = [(0, 1), (1, 0)]
COST = 30 * 10**9


def dot(a, b, ca, cb):
    return lax.dot_general(
        a, b, (((ca,), (cb,)), ((), ())), preferred_element_type=jnp.float32
    )


def exchange(blocks, axis):
    return lax.all_to_all(blocks, axis, split_axis=0, concat_axis=0, tiled=True)


def copies(block, n):
    return jnp.broadcast_to(block[None], (n, *block.shape))


def swap_in_block(x, step):
    return lax.ppermute(x, BLOCK, [(i, i ^ step) for i in range(4)])


VMEM = pl.BlockSpec(memory_space=pltpu.VMEM)
SMEM = pl.BlockSpec(memory_space=pltpu.SMEM)


def roomy(mib):
    return pltpu.CompilerParams(vmem_limit_bytes=mib * 2**20)


def lay_out_kernel(which, piece0, piece1, piece2, piece3, down, kept, given, down_kept, down_given):
    pieces = (piece0, piece1, piece2, piece3)
    units = kept.shape[0] // len(pieces)
    share = units // 2
    for side in range(2):

        @pl.when(which[0] == side)
        def _():
            for step, piece in enumerate(pieces):
                for kind in range(2):
                    turned = piece[kind].T
                    at = step * units + kind * share
                    near, far = side * share, (1 - side) * share
                    kept[at : at + share, :] = turned[near : near + share]
                    given[at : at + share, :] = turned[far : far + share]
            both = down[...]
            groups = both.shape[1] // units
            for out, half in ((down_kept, side), (down_given, 1 - side)):
                out[...] = jnp.concatenate(
                    [
                        both[:, g * units + half * share : g * units + (half + 1) * share]
                        for g in range(groups)
                    ],
                    axis=1,
                )


def lay_out(which, pieces, down):
    part, units = pieces[0].shape[1:]
    width, hidden = down.shape
    of = jax.ShapeDtypeStruct
    return pl.pallas_call(
        lay_out_kernel,
        out_shape=(
            of((len(pieces) * units, part), down.dtype),
            of((len(pieces) * units, part), down.dtype),
            of((width, hidden // 2), down.dtype),
            of((width, hidden // 2), down.dtype),
        ),
        in_specs=[SMEM] + [VMEM] * 5,
        out_specs=(VMEM,) * 4,
        compiler_params=roomy(16),
        cost_estimate=pl.CostEstimate(flops=COST, transcendentals=0, bytes_accessed=8 * 2**20),
    )(which, *pieces, down)


def down_kernel(partial, weight, hidden, out):
    total = partial[...] + dot(weight[...], hidden[...], 1, 0)
    out[...] = total.T.astype(out.dtype)


def down_product(partial, weight, hidden):
    return pl.pallas_call(
        down_kernel,
        out_shape=jax.ShapeDtypeStruct(partial.shape[::-1], jnp.bfloat16),
        in_specs=[VMEM] * 3,
        out_specs=VMEM,
        compiler_params=roomy(16),
    )(partial, weight, hidden)


def reorder_kernel(permutation, rows, out):
    out[...] = dot(permutation[...], rows[...], 1, 0).astype(out.dtype)


def reorder(permutation, rows):
    return pl.pallas_call(
        reorder_kernel,
        out_shape=jax.ShapeDtypeStruct(rows.shape, rows.dtype),
        in_specs=[VMEM] * 2,
        out_specs=VMEM,
        compiler_params=roomy(16),
    )(permutation, rows)


def combine_kernel(back, table, out):
    owners, rows, width = back.shape
    own = table.shape[0]
    groups = rows // own
    weight = jnp.concatenate([table[...]] * groups, axis=0)
    total = back[0].astype(jnp.float32) * weight[:, :1]
    for owner in range(1, owners):
        total = total + back[owner].astype(jnp.float32) * weight[:, owner : owner + 1]
    wide = jnp.concatenate([total[g * own : (g + 1) * own] for g in range(groups)], axis=1)
    out[...] = wide.astype(out.dtype)


def combine(back, table):
    owners, rows, width = back.shape
    own = table.shape[0]
    return pl.pallas_call(
        combine_kernel,
        out_shape=jax.ShapeDtypeStruct((own, rows // own * width), jnp.bfloat16),
        in_specs=[VMEM] * 2,
        out_specs=VMEM,
        compiler_params=roomy(16),
    )(back, table)


def per_device(tokens, expert_ids, scores, gate_weight, up_weight, down_weight):
    across = lax.axis_size(BLOCK)
    groups = lax.axis_size(GRP)
    owners = lax.axis_size("ex")
    side, col = lax.axis_index("side"), lax.axis_index(BLOCK)
    own, half_width = tokens.shape
    share = gate_weight.shape[2] // 2
    out_width = down_weight.shape[2]
    rows = own * owners
    total = rows * groups
    part = half_width // across

    lifted = jax.nn.sigmoid(scores)
    route_weight = 2.5 * lifted / jnp.sum(lifted, axis=-1, keepdims=True)
    named = expert_ids[:, :, None] == jnp.arange(owners, dtype=jnp.int32)
    table = jnp.sum(jnp.where(named, route_weight[:, :, None], 0.0), axis=1)
    index = jnp.arange(total, dtype=jnp.int32)
    source = (index // own) % groups * rows + index // (groups * own) * own + index % own
    permutation = (source[:, None] == index[None, :]).astype(jnp.bfloat16)

    def rows_of(step):
        start = (col ^ step) * part
        return jnp.stack(
            [lax.dynamic_slice_in_dim(w[0], start, part, 0) for w in (gate_weight, up_weight)]
        )

    pieces = [rows_of(0)] + [swap_in_block(rows_of(d), d) for d in range(1, across)]

    column = exchange(copies(tokens.reshape(-1, 4, 128), owners), "ex").reshape(rows, half_width)
    parts = jnp.transpose(column.reshape(rows, across, part), (1, 0, 2))
    parts, table, permutation = lax.optimization_barrier((parts, table, permutation))
    fan = jnp.broadcast_to(
        parts.reshape(1, 2, 1, 2, rows, part), (2, 2, 2, 2, rows, part)
    ).reshape(groups, rows, part)
    everyone = exchange(fan, GRP)
    kept, given, down_kept, down_given = lay_out(side.reshape(1), pieces, down_weight[0].T)
    everyone, kept, given, down_kept, down_given = lax.optimization_barrier(
        (everyone, kept, given, down_kept, down_given)
    )
    everyone = everyone.reshape(total, part)

    outgoing = dot(given, everyone, 1, 1).astype(jnp.bfloat16)
    arrived = lax.ppermute(outgoing, "side", SWAP)
    partial = lax.optimization_barrier(dot(kept, everyone, 1, 1))
    sums = (partial + arrived.astype(jnp.float32)).reshape(across, 2 * share, total)
    summed = sums[0]
    for d in (3, 1, 2):
        summed = summed + swap_in_block(sums[d].astype(jnp.bfloat16), d).astype(jnp.float32)
    hidden = (jax.nn.silu(summed[:share]) * summed[share:]).astype(jnp.bfloat16)

    mine = exchange(copies(hidden, groups), GRP).reshape(groups * share, total)
    other = lax.ppermute(mine, "side", SWAP)
    expert_out = down_product(dot(down_kept, mine, 1, 0), down_given, other)

    by_group = exchange(expert_out.reshape(groups, rows, out_width), GRP).reshape(total, out_width)
    turned = reorder(permutation, by_group)
    turned, table = lax.optimization_barrier((turned, table))
    back = exchange(turned.reshape(owners, groups * own, out_width), "ex")
    return combine(back, table)


def solution(mesh):
    sides, groups, owners = mesh.devices.shape
    names = ("side", *GRP, "ex")
    fine = Mesh(mesh.devices.reshape(sides, 2, 2, 2, groups // 8, owners), names)
    in_specs = (
        P((*GRP, "ex"), "side"),
        P((*GRP, "ex"), None),
        P((*GRP, "ex"), None),
        P("ex", "side", GRP),
        P("ex", "side", GRP),
        P("ex", None, ("side", *GRP)),
    )
    out_specs = P((*GRP, "ex"), "side")
    return jax.shard_map(
        per_device, mesh=fine, in_specs=in_specs, out_specs=out_specs, check_vma=False
    )
```

```python
import functools

import jax
import jax.numpy as jnp
from jax import lax
from jax.experimental import pallas as pl
from jax.experimental.pallas import tpu as pltpu
from jax.sharding import Mesh
from jax.sharding import PartitionSpec as P

GRP = ("yh", "yl", "xh", "xl")
BLOCK = ("yl", "xl")
SWAP = [(0, 1), (1, 0)]
COST = 30 * 10**9


def dot(a, b, ca, cb):
    return lax.dot_general(
        a, b, (((ca,), (cb,)), ((), ())), preferred_element_type=jnp.float32
    )


def exchange(blocks, axis):
    return lax.all_to_all(blocks, axis, split_axis=0, concat_axis=0, tiled=True)


def copies(block, n):
    return jnp.broadcast_to(block[None], (n, *block.shape))


def swap_in_block(x, step):
    return lax.ppermute(x, BLOCK, [(i, i ^ step) for i in range(4)])


VMEM = pl.BlockSpec(memory_space=pltpu.VMEM)
SMEM = pl.BlockSpec(memory_space=pltpu.SMEM)
HBM = pl.BlockSpec(memory_space=pltpu.HBM)


def roomy(mib):
    return pltpu.CompilerParams(vmem_limit_bytes=mib * 2**20)


def cut_kernel(place, gate, up, *refs):
    outs, sems = refs[:-1], refs[-1]
    part = outs[0].shape[1]
    moves = []
    for step, out in enumerate(outs):
        rows = pl.ds(pl.multiple_of((place[0] ^ step) * part, part), part)
        for kind, weight in enumerate((gate, up)):
            moves.append(
                pltpu.make_async_copy(weight.at[0, rows], out.at[kind], sems.at[2 * step + kind])
            )
    for move in moves:
        move.start()
    for move in moves:
        move.wait()


def cut(place, gate, up, across):
    part = gate.shape[1] // across
    shape = jax.ShapeDtypeStruct((2, part, gate.shape[2]), gate.dtype)
    return pl.pallas_call(
        cut_kernel,
        out_shape=(shape,) * across,
        in_specs=[SMEM, HBM, HBM],
        out_specs=(HBM,) * across,
        scratch_shapes=[pltpu.SemaphoreType.DMA((2 * across,))],
    )(place, gate, up)


def pass_kernel(*refs):
    del refs


def pass_through(arrays):
    n = len(arrays)
    return pl.pallas_call(
        pass_kernel,
        out_shape=tuple(jax.ShapeDtypeStruct(a.shape, a.dtype) for a in arrays),
        in_specs=[HBM] * n,
        out_specs=(HBM,) * n,
        input_output_aliases={i: i for i in range(n)},
        cost_estimate=pl.CostEstimate(flops=COST, transcendentals=0, bytes_accessed=8 * 2**20),
    )(*arrays)


def gate_up_kernel(kept, which, tokens, piece0, piece1, piece2, piece3, out):
    share = piece0.shape[2] // 2
    for side in range(2):
        first = (side if kept else 1 - side) * share
        units = slice(first, first + share)

        @pl.when(which[0] == side)
        def _():
            weight = jnp.concatenate(
                [p[kind, :, units] for p in (piece0, piece1, piece2, piece3) for kind in range(2)],
                axis=1,
            )
            out[...] = dot(weight, tokens[...], 0, 1).astype(out.dtype)


def gate_up(kept, which, tokens, pieces):
    units = pieces[0].shape[2]
    dtype = jnp.float32 if kept else jnp.bfloat16
    return pl.pallas_call(
        functools.partial(gate_up_kernel, kept),
        out_shape=jax.ShapeDtypeStruct((len(pieces) * units, tokens.shape[0]), dtype),
        in_specs=[SMEM] + [VMEM] * 5,
        out_specs=VMEM,
        compiler_params=roomy(16),
    )(which, tokens, *pieces)


def lay_out_kernel(which, down, down_kept, down_given):
    groups = 16
    units = down.shape[1] // groups
    share = units // 2
    for side in range(2):

        @pl.when(which[0] == side)
        def _():
            for out, half in ((down_kept, side), (down_given, 1 - side)):
                firsts = [g * units + half * share for g in range(groups)]
                out[...] = jnp.concatenate([down[:, f : f + share] for f in firsts], axis=1)


def lay_out(which, down):
    width, hidden = down.shape
    half = jax.ShapeDtypeStruct((width, hidden // 2), down.dtype)
    return pl.pallas_call(
        lay_out_kernel,
        out_shape=(half, half),
        in_specs=[SMEM, VMEM],
        out_specs=(VMEM, VMEM),
        compiler_params=roomy(16),
    )(which, down)


def down_kernel(partial, weight, hidden, out):
    total = partial[...] + dot(weight[...], hidden[...], 1, 0)
    out[...] = total.T.astype(out.dtype)


def down_product(partial, weight, hidden):
    return pl.pallas_call(
        down_kernel,
        out_shape=jax.ShapeDtypeStruct(partial.shape[::-1], jnp.bfloat16),
        in_specs=[VMEM] * 3,
        out_specs=VMEM,
        compiler_params=roomy(16),
    )(partial, weight, hidden)


def reorder_kernel(permutation, rows, out):
    out[...] = dot(permutation[...], rows[...], 1, 0).astype(out.dtype)


def reorder(permutation, rows):
    return pl.pallas_call(
        reorder_kernel,
        out_shape=jax.ShapeDtypeStruct(rows.shape, rows.dtype),
        in_specs=[VMEM] * 2,
        out_specs=VMEM,
        compiler_params=roomy(16),
    )(permutation, rows)


def combine_kernel(back, table, out):
    owners, rows, width = back.shape
    own = table.shape[0]
    groups = rows // own
    weight = jnp.concatenate([table[...]] * groups, axis=0)
    total = back[0].astype(jnp.float32) * weight[:, :1]
    for owner in range(1, owners):
        total = total + back[owner].astype(jnp.float32) * weight[:, owner : owner + 1]
    wide = jnp.concatenate([total[g * own : (g + 1) * own] for g in range(groups)], axis=1)
    out[...] = wide.astype(out.dtype)


def combine(back, table):
    owners, rows, width = back.shape
    own = table.shape[0]
    return pl.pallas_call(
        combine_kernel,
        out_shape=jax.ShapeDtypeStruct((own, rows // own * width), jnp.bfloat16),
        in_specs=[VMEM] * 2,
        out_specs=VMEM,
        compiler_params=roomy(16),
    )(back, table)


def per_device(tokens, expert_ids, scores, gate_weight, up_weight, down_weight):
    across = lax.axis_size(BLOCK)
    groups = lax.axis_size(GRP)
    owners = lax.axis_size("ex")
    side, col = lax.axis_index("side"), lax.axis_index(BLOCK)
    own, half_width = tokens.shape
    share = gate_weight.shape[2] // 2
    out_width = down_weight.shape[2]
    rows = own * owners
    total = rows * groups
    part = half_width // across

    lifted = jax.nn.sigmoid(scores)
    route_weight = 2.5 * lifted / jnp.sum(lifted, axis=-1, keepdims=True)
    named = expert_ids[:, :, None] == jnp.arange(owners, dtype=jnp.int32)
    table = jnp.sum(jnp.where(named, route_weight[:, :, None], 0.0), axis=1)
    index = jnp.arange(total, dtype=jnp.int32)
    source = (index // own) % groups * rows + index // (groups * own) * own + index % own
    permutation = (source[:, None] == index[None, :]).astype(jnp.bfloat16)

    shares = cut(col.reshape(1), gate_weight, up_weight, across)
    pieces = [shares[0]] + [swap_in_block(shares[d], d) for d in range(1, across)]

    column = exchange(copies(tokens.reshape(-1, 4, 128), owners), "ex").reshape(rows, half_width)
    parts = jnp.transpose(column.reshape(rows, across, part), (1, 0, 2))
    parts, table, permutation = lax.optimization_barrier((parts, table, permutation))
    fan = jnp.broadcast_to(
        parts.reshape(1, 2, 1, 2, rows, part), (2, 2, 2, 2, rows, part)
    ).reshape(groups, rows, part)
    everyone = exchange(fan, GRP)
    pieces = [pieces[0], *pass_through(pieces[1:])]
    which = side.reshape(1)
    down_kept, down_given = lay_out(which, down_weight[0].T)
    everyone, pieces, down_kept, down_given = lax.optimization_barrier(
        (everyone, pieces, down_kept, down_given)
    )
    everyone = everyone.reshape(total, part)

    outgoing = gate_up(False, which, everyone, pieces)
    arrived = lax.ppermute(outgoing, "side", SWAP)
    partial = gate_up(True, which, everyone, pieces)
    sums = (partial + arrived.astype(jnp.float32)).reshape(across, 2 * share, total)
    summed = sums[0]
    for d in (3, 1, 2):
        summed = summed + swap_in_block(sums[d].astype(jnp.bfloat16), d).astype(jnp.float32)
    hidden = (jax.nn.silu(summed[:share]) * summed[share:]).astype(jnp.bfloat16)

    mine = exchange(copies(hidden, groups), GRP).reshape(groups * share, total)
    other = lax.ppermute(mine, "side", SWAP)
    expert_out = down_product(dot(down_kept, mine, 1, 0), down_given, other)

    by_group = exchange(expert_out.reshape(groups, rows, out_width), GRP).reshape(total, out_width)
    turned = reorder(permutation, by_group)
    turned, table = lax.optimization_barrier((turned, table))
    back = exchange(turned.reshape(owners, groups * own, out_width), "ex")
    return combine(back, table)


def solution(mesh):
    sides, groups, owners = mesh.devices.shape
    names = ("side", *GRP, "ex")
    fine = Mesh(mesh.devices.reshape(sides, 2, 2, 2, groups // 8, owners), names)
    in_specs = (
        P((*GRP, "ex"), "side"),
        P((*GRP, "ex"), None),
        P((*GRP, "ex"), None),
        P("ex", "side", GRP),
        P("ex", "side", GRP),
        P("ex", None, ("side", *GRP)),
    )
    out_specs = P((*GRP, "ex"), "side")
    return jax.shard_map(
        per_device, mesh=fine, in_specs=in_specs, out_specs=out_specs, check_vma=False
    )
```

```python
import jax
import jax.numpy as jnp
from jax import lax
from jax.experimental import pallas as pl
from jax.experimental.pallas import tpu as pltpu
from jax.sharding import Mesh
from jax.sharding import PartitionSpec as P

GRP = ("yh", "yl", "xh", "xl")
BLOCK = ("yl", "xl")
SWAP = [(0, 1), (1, 0)]
COST = 30 * 10**9


def dot(a, b, ca, cb):
    return lax.dot_general(
        a, b, (((ca,), (cb,)), ((), ())), preferred_element_type=jnp.float32
    )


def exchange(blocks, axis):
    return lax.all_to_all(blocks, axis, split_axis=0, concat_axis=0, tiled=True)


def copies(block, n):
    return jnp.broadcast_to(block[None], (n, *block.shape))


def swap_in_block(x, step):
    return lax.ppermute(x, BLOCK, [(i, i ^ step) for i in range(4)])


VMEM = pl.BlockSpec(memory_space=pltpu.VMEM)
SMEM = pl.BlockSpec(memory_space=pltpu.SMEM)
HBM = pl.BlockSpec(memory_space=pltpu.HBM)


def roomy(mib):
    return pltpu.CompilerParams(vmem_limit_bytes=mib * 2**20)


def cut_kernel(place, gate, up, *refs):
    outs, sems = refs[:-1], refs[-1]
    part = outs[0].shape[1]
    moves = []
    for step, out in enumerate(outs):
        rows = pl.ds(pl.multiple_of((place[0] ^ step) * part, part), part)
        for kind, weight in enumerate((gate, up)):
            moves.append(
                pltpu.make_async_copy(weight.at[0, rows], out.at[kind], sems.at[2 * step + kind])
            )
    for move in moves:
        move.start()
    for move in moves:
        move.wait()


def cut(place, gate, up, across):
    part = gate.shape[1] // across
    shape = jax.ShapeDtypeStruct((2, part, gate.shape[2]), gate.dtype)
    return pl.pallas_call(
        cut_kernel,
        out_shape=(shape,) * across,
        in_specs=[SMEM, HBM, HBM],
        out_specs=(VMEM,) * across,
        scratch_shapes=[pltpu.SemaphoreType.DMA((2 * across,))],
        compiler_params=roomy(16),
    )(place, gate, up)


def lay_out_kernel(which, piece0, piece1, piece2, piece3, down, kept, given, down_kept, down_given):
    pieces = (piece0, piece1, piece2, piece3)
    units = kept.shape[0] // len(pieces)
    share = units // 2
    for side in range(2):

        @pl.when(which[0] == side)
        def _():
            for step, piece in enumerate(pieces):
                for kind in range(2):
                    turned = piece[kind].T
                    at = step * units + kind * share
                    near, far = side * share, (1 - side) * share
                    kept[at : at + share, :] = turned[near : near + share]
                    given[at : at + share, :] = turned[far : far + share]
            both = down[...]
            groups = both.shape[1] // units
            for out, half in ((down_kept, side), (down_given, 1 - side)):
                out[...] = jnp.concatenate(
                    [
                        both[:, g * units + half * share : g * units + (half + 1) * share]
                        for g in range(groups)
                    ],
                    axis=1,
                )


def lay_out(which, pieces, down):
    part, units = pieces[0].shape[1:]
    width, hidden = down.shape
    of = jax.ShapeDtypeStruct
    return pl.pallas_call(
        lay_out_kernel,
        out_shape=(
            of((len(pieces) * units, part), down.dtype),
            of((len(pieces) * units, part), down.dtype),
            of((width, hidden // 2), down.dtype),
            of((width, hidden // 2), down.dtype),
        ),
        in_specs=[SMEM] + [VMEM] * 5,
        out_specs=(VMEM,) * 4,
        compiler_params=roomy(16),
        cost_estimate=pl.CostEstimate(flops=COST, transcendentals=0, bytes_accessed=8 * 2**20),
    )(which, *pieces, down)


def product_kernel(weight, tokens, out):
    out[...] = dot(weight[...], tokens[...], 1, 1).astype(out.dtype)


def product(weight, tokens, dtype):
    return pl.pallas_call(
        product_kernel,
        out_shape=jax.ShapeDtypeStruct((weight.shape[0], tokens.shape[0]), dtype),
        in_specs=[VMEM] * 2,
        out_specs=VMEM,
        compiler_params=roomy(16),
    )(weight, tokens)


def down_kernel(partial, weight, hidden, out):
    total = partial[...] + dot(weight[...], hidden[...], 1, 0)
    out[...] = total.T.astype(out.dtype)


def down_product(partial, weight, hidden):
    return pl.pallas_call(
        down_kernel,
        out_shape=jax.ShapeDtypeStruct(partial.shape[::-1], jnp.bfloat16),
        in_specs=[VMEM] * 3,
        out_specs=VMEM,
        compiler_params=roomy(16),
    )(partial, weight, hidden)


def reorder_kernel(permutation, rows, out):
    out[...] = dot(permutation[...], rows[...], 1, 0).astype(out.dtype)


def reorder(permutation, rows):
    return pl.pallas_call(
        reorder_kernel,
        out_shape=jax.ShapeDtypeStruct(rows.shape, rows.dtype),
        in_specs=[VMEM] * 2,
        out_specs=VMEM,
        compiler_params=roomy(16),
    )(permutation, rows)


def combine_kernel(back, table, out):
    owners, rows, width = back.shape
    own = table.shape[0]
    groups = rows // own
    weight = jnp.concatenate([table[...]] * groups, axis=0)
    total = back[0].astype(jnp.float32) * weight[:, :1]
    for owner in range(1, owners):
        total = total + back[owner].astype(jnp.float32) * weight[:, owner : owner + 1]
    wide = jnp.concatenate([total[g * own : (g + 1) * own] for g in range(groups)], axis=1)
    out[...] = wide.astype(out.dtype)


def combine(back, table):
    owners, rows, width = back.shape
    own = table.shape[0]
    return pl.pallas_call(
        combine_kernel,
        out_shape=jax.ShapeDtypeStruct((own, rows // own * width), jnp.bfloat16),
        in_specs=[VMEM] * 2,
        out_specs=VMEM,
        compiler_params=roomy(16),
    )(back, table)


def per_device(tokens, expert_ids, scores, gate_weight, up_weight, down_weight):
    across = lax.axis_size(BLOCK)
    groups = lax.axis_size(GRP)
    owners = lax.axis_size("ex")
    side, col = lax.axis_index("side"), lax.axis_index(BLOCK)
    own, half_width = tokens.shape
    share = gate_weight.shape[2] // 2
    out_width = down_weight.shape[2]
    rows = own * owners
    total = rows * groups
    part = half_width // across

    lifted = jax.nn.sigmoid(scores)
    route_weight = 2.5 * lifted / jnp.sum(lifted, axis=-1, keepdims=True)
    named = expert_ids[:, :, None] == jnp.arange(owners, dtype=jnp.int32)
    table = jnp.sum(jnp.where(named, route_weight[:, :, None], 0.0), axis=1)
    index = jnp.arange(total, dtype=jnp.int32)
    source = (index // own) % groups * rows + index // (groups * own) * own + index % own
    permutation = (source[:, None] == index[None, :]).astype(jnp.bfloat16)

    shares = cut(col.reshape(1), gate_weight, up_weight, across)
    pieces = [shares[0]] + [swap_in_block(shares[d], d) for d in range(1, across)]

    column = exchange(copies(tokens.reshape(-1, 4, 128), owners), "ex").reshape(rows, half_width)
    parts = jnp.transpose(column.reshape(rows, across, part), (1, 0, 2))
    parts, table, permutation = lax.optimization_barrier((parts, table, permutation))
    fan = jnp.broadcast_to(
        parts.reshape(1, 2, 1, 2, rows, part), (2, 2, 2, 2, rows, part)
    ).reshape(groups, rows, part)
    everyone = exchange(fan, GRP)
    kept, given, down_kept, down_given = lay_out(side.reshape(1), pieces, down_weight[0].T)
    everyone, kept, given, down_kept, down_given = lax.optimization_barrier(
        (everyone, kept, given, down_kept, down_given)
    )
    everyone = everyone.reshape(total, part)

    outgoing = product(given, everyone, jnp.bfloat16)
    arrived = lax.ppermute(outgoing, "side", SWAP)
    partial = product(kept, everyone, jnp.float32)
    sums = (partial + arrived.astype(jnp.float32)).reshape(across, 2 * share, total)
    summed = sums[0]
    for d in (3, 1, 2):
        summed = summed + swap_in_block(sums[d].astype(jnp.bfloat16), d).astype(jnp.float32)
    hidden = (jax.nn.silu(summed[:share]) * summed[share:]).astype(jnp.bfloat16)

    mine = exchange(copies(hidden, groups), GRP).reshape(groups * share, total)
    other = lax.ppermute(mine, "side", SWAP)
    expert_out = down_product(dot(down_kept, mine, 1, 0), down_given, other)

    by_group = exchange(expert_out.reshape(groups, rows, out_width), GRP).reshape(total, out_width)
    turned = reorder(permutation, by_group)
    turned, table = lax.optimization_barrier((turned, table))
    back = exchange(turned.reshape(owners, groups * own, out_width), "ex")
    return combine(back, table)


def solution(mesh):
    sides, groups, owners = mesh.devices.shape
    names = ("side", *GRP, "ex")
    fine = Mesh(mesh.devices.reshape(sides, 2, 2, 2, groups // 8, owners), names)
    in_specs = (
        P((*GRP, "ex"), "side"),
        P((*GRP, "ex"), None),
        P((*GRP, "ex"), None),
        P("ex", "side", GRP),
        P("ex", "side", GRP),
        P("ex", None, ("side", *GRP)),
    )
    out_specs = P((*GRP, "ex"), "side")
    return jax.shard_map(
        per_device, mesh=fine, in_specs=in_specs, out_specs=out_specs, check_vma=False
    )
```

```python
import jax
import jax.numpy as jnp
from jax import lax
from jax.experimental import pallas as pl
from jax.experimental.pallas import tpu as pltpu
from jax.sharding import Mesh
from jax.sharding import PartitionSpec as P

GRP = ("yh", "yl", "xh", "xl")
BLOCK = ("yl", "xl")
SWAP = [(0, 1), (1, 0)]
COST = 30 * 10**9
SHARE = 64


def dot(a, b, ca, cb):
    return lax.dot_general(
        a, b, (((ca,), (cb,)), ((), ())), preferred_element_type=jnp.float32
    )


def exchange(blocks, axis):
    return lax.all_to_all(blocks, axis, split_axis=0, concat_axis=0, tiled=True)


def copies(block, n):
    return jnp.broadcast_to(block[None], (n, *block.shape))


def swap_in_block(x, step):
    return lax.ppermute(x, BLOCK, [(i, i ^ step) for i in range(4)])


VMEM = pl.BlockSpec(memory_space=pltpu.VMEM)
SMEM = pl.BlockSpec(memory_space=pltpu.SMEM)
HBM = pl.BlockSpec(memory_space=pltpu.HBM)


def roomy(mib):
    return pltpu.CompilerParams(vmem_limit_bytes=mib * 2**20)


def turn_kernel(which, piece0, piece1, piece2, piece3, kept, given, held, sems):
    pieces = (piece0, piece1, piece2, piece3)
    units = held.shape[3]
    share = units // 2
    moves = [
        pltpu.make_async_copy(piece, held.at[step], sems.at[step])
        for step, piece in enumerate(pieces)
    ]
    for move in moves:
        move.start()
    for step, move in enumerate(moves):
        move.wait()
        for side in range(2):

            @pl.when(which[0] == side)
            def _():
                for kind in range(2):
                    turned = held[step, kind].T
                    at = step * units + kind * share
                    near, far = side * share, (1 - side) * share
                    kept[at : at + share, :] = turned[near : near + share]
                    given[at : at + share, :] = turned[far : far + share]


def turn(which, pieces):
    part, units = pieces[0].shape[1:]
    dtype = pieces[0].dtype
    half = jax.ShapeDtypeStruct((len(pieces) * units, part), dtype)
    return pl.pallas_call(
        turn_kernel,
        out_shape=(half, half),
        in_specs=[SMEM] + [HBM] * 4,
        out_specs=(VMEM, VMEM),
        scratch_shapes=[
            pltpu.VMEM((len(pieces), *pieces[0].shape), dtype),
            pltpu.SemaphoreType.DMA((len(pieces),)),
        ],
        compiler_params=roomy(58),
        cost_estimate=pl.CostEstimate(flops=COST, transcendentals=0, bytes_accessed=4 * 2**20),
    )(which, *pieces)


def split_kernel(which, down, down_kept, down_given):
    groups = down.shape[1] // (2 * SHARE)
    for side in range(2):

        @pl.when(which[0] == side)
        def _():
            for out, half in ((down_kept, side), (down_given, 1 - side)):
                firsts = [(2 * g + half) * SHARE for g in range(groups)]
                out[...] = jnp.concatenate([down[:, f : f + SHARE] for f in firsts], axis=1)


def split(which, down):
    width, hidden = down.shape
    half = jax.ShapeDtypeStruct((width, hidden // 2), down.dtype)
    return pl.pallas_call(
        split_kernel,
        out_shape=(half, half),
        in_specs=[SMEM, VMEM],
        out_specs=(VMEM, VMEM),
        compiler_params=roomy(16),
    )(which, down)


def product_kernel(weight, tokens, out):
    out[...] = dot(weight[...], tokens[...], 1, 1).astype(out.dtype)


def product(weight, tokens, dtype):
    return pl.pallas_call(
        product_kernel,
        out_shape=jax.ShapeDtypeStruct((weight.shape[0], tokens.shape[0]), dtype),
        in_specs=[VMEM] * 2,
        out_specs=VMEM,
        compiler_params=roomy(16),
    )(weight, tokens)


def down_kernel(partial, weight, hidden, out):
    total = partial[...] + dot(weight[...], hidden[...], 1, 0)
    out[...] = total.T.astype(out.dtype)


def down_product(partial, weight, hidden):
    return pl.pallas_call(
        down_kernel,
        out_shape=jax.ShapeDtypeStruct(partial.shape[::-1], jnp.bfloat16),
        in_specs=[VMEM] * 3,
        out_specs=VMEM,
        compiler_params=roomy(16),
    )(partial, weight, hidden)


def reorder_kernel(permutation, rows, out):
    out[...] = dot(permutation[...], rows[...], 1, 0).astype(out.dtype)


def reorder(permutation, rows):
    return pl.pallas_call(
        reorder_kernel,
        out_shape=jax.ShapeDtypeStruct(rows.shape, rows.dtype),
        in_specs=[VMEM] * 2,
        out_specs=VMEM,
        compiler_params=roomy(16),
    )(permutation, rows)


def combine_kernel(back, table, out):
    owners, rows, width = back.shape
    own = table.shape[0]
    groups = rows // own
    weight = jnp.concatenate([table[...]] * groups, axis=0)
    total = back[0].astype(jnp.float32) * weight[:, :1]
    for owner in range(1, owners):
        total = total + back[owner].astype(jnp.float32) * weight[:, owner : owner + 1]
    wide = jnp.concatenate([total[g * own : (g + 1) * own] for g in range(groups)], axis=1)
    out[...] = wide.astype(out.dtype)


def combine(back, table):
    owners, rows, width = back.shape
    own = table.shape[0]
    return pl.pallas_call(
        combine_kernel,
        out_shape=jax.ShapeDtypeStruct((own, rows // own * width), jnp.bfloat16),
        in_specs=[VMEM] * 2,
        out_specs=VMEM,
        compiler_params=roomy(16),
    )(back, table)


def per_device(tokens, expert_ids, scores, gate_weight, up_weight, down_weight):
    across = lax.axis_size(BLOCK)
    groups = lax.axis_size(GRP)
    owners = lax.axis_size("ex")
    side, col = lax.axis_index("side"), lax.axis_index(BLOCK)
    own, half_width = tokens.shape
    share = gate_weight.shape[2] // 2
    out_width = down_weight.shape[2]
    rows = own * owners
    total = rows * groups
    part = half_width // across

    lifted = jax.nn.sigmoid(scores)
    route_weight = 2.5 * lifted / jnp.sum(lifted, axis=-1, keepdims=True)
    named = expert_ids[:, :, None] == jnp.arange(owners, dtype=jnp.int32)
    table = jnp.sum(jnp.where(named, route_weight[:, :, None], 0.0), axis=1)
    def rows_of(step):
        start = (col ^ step) * part
        return jnp.stack(
            [lax.dynamic_slice_in_dim(w[0], start, part, 0) for w in (gate_weight, up_weight)]
        )

    pieces = [rows_of(0)] + [swap_in_block(rows_of(d), d) for d in range(1, across)]

    column = exchange(copies(tokens.reshape(-1, 4, 128), owners), "ex").reshape(rows, half_width)
    parts = jnp.transpose(column.reshape(rows, across, part), (1, 0, 2))
    parts, table = lax.optimization_barrier((parts, table))
    fan = jnp.broadcast_to(
        parts.reshape(1, 2, 1, 2, rows, part), (2, 2, 2, 2, rows, part)
    ).reshape(groups, rows, part)
    everyone = exchange(fan, GRP)
    which = side.reshape(1)
    kept, given = turn(which, pieces)
    everyone, kept, given = lax.optimization_barrier((everyone, kept, given))
    everyone = everyone.reshape(total, part)

    outgoing = product(given, everyone, jnp.bfloat16)
    arrived = lax.ppermute(outgoing, "side", SWAP)
    partial = product(kept, everyone, jnp.float32)
    sums = (partial + arrived.astype(jnp.float32)).reshape(across, 2 * share, total)
    summed = sums[0]
    for d in (3, 1, 2):
        summed = summed + swap_in_block(sums[d].astype(jnp.bfloat16), d).astype(jnp.float32)
    hidden = (jax.nn.silu(summed[:share]) * summed[share:]).astype(jnp.bfloat16)

    mine = exchange(copies(hidden, groups), GRP).reshape(groups * share, total)
    mine, which, index = lax.optimization_barrier(
        (mine, which, jnp.arange(total, dtype=jnp.int32))
    )
    other = lax.ppermute(mine, "side", SWAP)
    down_kept, down_given = split(which, down_weight[0].T)
    source = (index // own) % groups * rows + index // (groups * own) * own + index % own
    permutation = (source[:, None] == index[None, :]).astype(jnp.bfloat16)
    partial = dot(down_kept, mine, 1, 0)
    partial, permutation, other = lax.optimization_barrier((partial, permutation, other))
    expert_out = down_product(partial, down_given, other)

    by_group = exchange(expert_out.reshape(groups, rows, out_width), GRP).reshape(total, out_width)
    turned = reorder(permutation, by_group)
    turned, table = lax.optimization_barrier((turned, table))
    back = exchange(turned.reshape(owners, groups * own, out_width), "ex")
    return combine(back, table)


def solution(mesh):
    sides, groups, owners = mesh.devices.shape
    names = ("side", *GRP, "ex")
    fine = Mesh(mesh.devices.reshape(sides, 2, 2, 2, groups // 8, owners), names)
    in_specs = (
        P((*GRP, "ex"), "side"),
        P((*GRP, "ex"), None),
        P((*GRP, "ex"), None),
        P("ex", "side", GRP),
        P("ex", "side", GRP),
        P("ex", None, ("side", *GRP)),
    )
    out_specs = P((*GRP, "ex"), "side")
    return jax.shard_map(
        per_device, mesh=fine, in_specs=in_specs, out_specs=out_specs, check_vma=False
    )
```

```python
import jax
import jax.numpy as jnp
from jax import lax
from jax.experimental import pallas as pl
from jax.experimental.pallas import tpu as pltpu
from jax.sharding import Mesh
from jax.sharding import PartitionSpec as P

GRP = ("yh", "yl", "xh", "xl")
BLOCK = ("yl", "xl")
SWAP = [(0, 1), (1, 0)]
COST = 30 * 10**9
SHARE = 64


def dot(a, b, ca, cb):
    return lax.dot_general(
        a, b, (((ca,), (cb,)), ((), ())), preferred_element_type=jnp.float32
    )


def exchange(blocks, axis):
    return lax.all_to_all(blocks, axis, split_axis=0, concat_axis=0, tiled=True)


def copies(block, n):
    return jnp.broadcast_to(block[None], (n, *block.shape))


def swap_in_block(x, step):
    return lax.ppermute(x, BLOCK, [(i, i ^ step) for i in range(4)])


VMEM = pl.BlockSpec(memory_space=pltpu.VMEM)
SMEM = pl.BlockSpec(memory_space=pltpu.SMEM)
HBM = pl.BlockSpec(memory_space=pltpu.HBM)


def roomy(mib):
    return pltpu.CompilerParams(vmem_limit_bytes=mib * 2**20)


def turn_kernel(place, piece0, piece1, piece2, piece3, kept, given, held, sems):
    pieces = (piece0, piece1, piece2, piece3)
    units = held.shape[3]
    share = units // 2
    moves = [
        pltpu.make_async_copy(piece, held.at[step], sems.at[step])
        for step, piece in enumerate(pieces)
    ]
    for move in moves:
        move.start()
    for step, move in enumerate(moves):
        move.wait()
        first = pl.multiple_of((place[1] ^ step) * units, units)
        for side in range(2):

            @pl.when(place[0] == side)
            def _():
                for kind in range(2):
                    turned = held[step, kind].T
                    near, far = side * share, (1 - side) * share
                    rows = pl.ds(pl.multiple_of(first + kind * share, share), share)
                    kept[rows, :] = turned[near : near + share]
                    given[rows, :] = turned[far : far + share]


def turn(place, pieces):
    part, units = pieces[0].shape[1:]
    dtype = pieces[0].dtype
    half = jax.ShapeDtypeStruct((len(pieces) * units, part), dtype)
    return pl.pallas_call(
        turn_kernel,
        out_shape=(half, half),
        in_specs=[SMEM] + [HBM] * 4,
        out_specs=(VMEM, VMEM),
        scratch_shapes=[
            pltpu.VMEM((len(pieces), *pieces[0].shape), dtype),
            pltpu.SemaphoreType.DMA((len(pieces),)),
        ],
        compiler_params=roomy(58),
        cost_estimate=pl.CostEstimate(flops=COST, transcendentals=0, bytes_accessed=4 * 2**20),
    )(place, *pieces)


def split_kernel(which, down, down_kept, down_given):
    groups = down.shape[1] // (2 * SHARE)
    for side in range(2):

        @pl.when(which[0] == side)
        def _():
            for out, half in ((down_kept, side), (down_given, 1 - side)):
                firsts = [(2 * g + half) * SHARE for g in range(groups)]
                out[...] = jnp.concatenate([down[:, f : f + SHARE] for f in firsts], axis=1)


def split(which, down):
    width, hidden = down.shape
    half = jax.ShapeDtypeStruct((width, hidden // 2), down.dtype)
    return pl.pallas_call(
        split_kernel,
        out_shape=(half, half),
        in_specs=[SMEM, VMEM],
        out_specs=(VMEM, VMEM),
        compiler_params=roomy(16),
    )(which, down)


def product_kernel(weight, tokens, out):
    out[...] = dot(weight[...], tokens[...], 1, 1)


def product(weight, tokens):
    return pl.pallas_call(
        product_kernel,
        out_shape=jax.ShapeDtypeStruct((weight.shape[0], tokens.shape[0]), jnp.float32),
        in_specs=[VMEM] * 2,
        out_specs=VMEM,
        compiler_params=roomy(16),
    )(weight, tokens)


def product_onto_kernel(partial, weight, tokens, out):
    out[...] = (partial[...] + dot(weight[...], tokens[...], 1, 1)).astype(out.dtype)


def product_onto(partial, weight, tokens):
    return pl.pallas_call(
        product_onto_kernel,
        out_shape=jax.ShapeDtypeStruct(partial.shape, jnp.bfloat16),
        in_specs=[VMEM] * 3,
        out_specs=VMEM,
        compiler_params=roomy(16),
    )(partial, weight, tokens)


def down_kernel(partial, weight, hidden, out):
    total = partial[...] + dot(weight[...], hidden[...], 1, 0)
    out[...] = total.T.astype(out.dtype)


def down_product(partial, weight, hidden):
    return pl.pallas_call(
        down_kernel,
        out_shape=jax.ShapeDtypeStruct(partial.shape[::-1], jnp.bfloat16),
        in_specs=[VMEM] * 3,
        out_specs=VMEM,
        compiler_params=roomy(16),
    )(partial, weight, hidden)


def reorder_kernel(permutation, rows, out):
    out[...] = dot(permutation[...], rows[...], 1, 0).astype(out.dtype)


def reorder(permutation, rows):
    return pl.pallas_call(
        reorder_kernel,
        out_shape=jax.ShapeDtypeStruct(rows.shape, rows.dtype),
        in_specs=[VMEM] * 2,
        out_specs=VMEM,
        compiler_params=roomy(16),
    )(permutation, rows)


def combine_kernel(back, table, out):
    owners, rows, width = back.shape
    own = table.shape[0]
    groups = rows // own
    weight = jnp.concatenate([table[...]] * groups, axis=0)
    total = back[0].astype(jnp.float32) * weight[:, :1]
    for owner in range(1, owners):
        total = total + back[owner].astype(jnp.float32) * weight[:, owner : owner + 1]
    wide = jnp.concatenate([total[g * own : (g + 1) * own] for g in range(groups)], axis=1)
    out[...] = wide.astype(out.dtype)


def combine(back, table):
    owners, rows, width = back.shape
    own = table.shape[0]
    return pl.pallas_call(
        combine_kernel,
        out_shape=jax.ShapeDtypeStruct((own, rows // own * width), jnp.bfloat16),
        in_specs=[VMEM] * 2,
        out_specs=VMEM,
        compiler_params=roomy(16),
    )(back, table)


def per_device(tokens, expert_ids, scores, gate_weight, up_weight, down_weight):
    across = lax.axis_size(BLOCK)
    groups = lax.axis_size(GRP)
    owners = lax.axis_size("ex")
    side, col = lax.axis_index("side"), lax.axis_index(BLOCK)
    own, half_width = tokens.shape
    share = gate_weight.shape[2] // 2
    out_width = down_weight.shape[2]
    rows = own * owners
    total = rows * groups
    part = half_width // across

    lifted = jax.nn.sigmoid(scores)
    route_weight = 2.5 * lifted / jnp.sum(lifted, axis=-1, keepdims=True)
    named = expert_ids[:, :, None] == jnp.arange(owners, dtype=jnp.int32)
    table = jnp.sum(jnp.where(named, route_weight[:, :, None], 0.0), axis=1)
    def rows_of(step):
        start = (col ^ step) * part
        return jnp.stack(
            [lax.dynamic_slice_in_dim(w[0], start, part, 0) for w in (gate_weight, up_weight)]
        )

    pieces = [rows_of(0)] + [swap_in_block(rows_of(d), d) for d in range(1, across)]

    column = exchange(copies(tokens.reshape(-1, 4, 128), owners), "ex").reshape(rows, half_width)
    parts = jnp.transpose(column.reshape(rows, across, part), (1, 0, 2))
    parts, table = lax.optimization_barrier((parts, table))
    fan = jnp.broadcast_to(
        parts.reshape(1, 2, 1, 2, rows, part), (2, 2, 2, 2, rows, part)
    ).reshape(groups, rows, part)
    everyone = exchange(fan, GRP)
    which = side.reshape(1)
    kept, given = turn(jnp.stack([side, col]).astype(jnp.int32), pieces)
    given = lax.ppermute(given, "side", SWAP)
    everyone, kept, given = lax.optimization_barrier((everyone, kept, given))
    everyone = everyone.reshape(total, part)

    far = lax.ppermute(everyone, "side", SWAP)
    sums = product_onto(product(kept, everyone), given, far)
    sums = exchange(sums.reshape(across, 2 * share, total), BLOCK)
    summed = jnp.sum(sums.astype(jnp.float32), axis=0)
    hidden = (jax.nn.silu(summed[:share]) * summed[share:]).astype(jnp.bfloat16)

    mine = exchange(copies(hidden, groups), GRP).reshape(groups * share, total)
    mine, which, index = lax.optimization_barrier(
        (mine, which, jnp.arange(total, dtype=jnp.int32))
    )
    other = lax.ppermute(mine, "side", SWAP)
    down_kept, down_given = split(which, down_weight[0].T)
    source = (index // own) % groups * rows + index // (groups * own) * own + index % own
    permutation = (source[:, None] == index[None, :]).astype(jnp.bfloat16)
    partial = dot(down_kept, mine, 1, 0)
    partial, permutation, other = lax.optimization_barrier((partial, permutation, other))
    expert_out = down_product(partial, down_given, other)

    by_group = exchange(expert_out.reshape(groups, rows, out_width), GRP).reshape(total, out_width)
    turned = reorder(permutation, by_group)
    turned, table = lax.optimization_barrier((turned, table))
    back = exchange(turned.reshape(owners, groups * own, out_width), "ex")
    return combine(back, table)


def solution(mesh):
    sides, groups, owners = mesh.devices.shape
    names = ("side", *GRP, "ex")
    fine = Mesh(mesh.devices.reshape(sides, 2, 2, 2, groups // 8, owners), names)
    in_specs = (
        P((*GRP, "ex"), "side"),
        P((*GRP, "ex"), None),
        P((*GRP, "ex"), None),
        P("ex", "side", GRP),
        P("ex", "side", GRP),
        P("ex", None, ("side", *GRP)),
    )
    out_specs = P((*GRP, "ex"), "side")
    return jax.shard_map(
        per_device, mesh=fine, in_specs=in_specs, out_specs=out_specs, check_vma=False
    )
```

```python
import jax
import jax.numpy as jnp
from jax import lax
from jax.experimental import pallas as pl
from jax.experimental.pallas import tpu as pltpu
from jax.sharding import Mesh
from jax.sharding import PartitionSpec as P

GRP = ("yh", "yl", "xh", "xl")
BLOCK = ("yl", "xl")
SWAP = [(0, 1), (1, 0)]
COST = 30 * 10**9
SHARE = 64


def dot(a, b, ca, cb):
    return lax.dot_general(
        a, b, (((ca,), (cb,)), ((), ())), preferred_element_type=jnp.float32
    )


def exchange(blocks, axis):
    return lax.all_to_all(blocks, axis, split_axis=0, concat_axis=0, tiled=True)


def copies(block, n):
    return jnp.broadcast_to(block[None], (n, *block.shape))


def swap_in_block(x, step):
    return lax.ppermute(x, BLOCK, [(i, i ^ step) for i in range(4)])


VMEM = pl.BlockSpec(memory_space=pltpu.VMEM)
SMEM = pl.BlockSpec(memory_space=pltpu.SMEM)
HBM = pl.BlockSpec(memory_space=pltpu.HBM)


def roomy(mib):
    return pltpu.CompilerParams(vmem_limit_bytes=mib * 2**20)


def turn_kernel(place, piece0, piece1, piece2, piece3, kept, given, held, sems):
    pieces = (piece0, piece1, piece2, piece3)
    units = held.shape[3]
    share = units // 2
    moves = [
        pltpu.make_async_copy(piece, held.at[step], sems.at[step])
        for step, piece in enumerate(pieces)
    ]
    for move in moves:
        move.start()
    for step, move in enumerate(moves):
        move.wait()
        first = pl.multiple_of((place[1] ^ step) * units, units)
        for side in range(2):

            @pl.when(place[0] == side)
            def _():
                for kind in range(2):
                    turned = held[step, kind].T
                    near, far = side * share, (1 - side) * share
                    rows = pl.ds(pl.multiple_of(first + kind * share, share), share)
                    kept[rows, :] = turned[near : near + share]
                    given[rows, :] = turned[far : far + share]


def turn(place, pieces):
    part, units = pieces[0].shape[1:]
    dtype = pieces[0].dtype
    half = jax.ShapeDtypeStruct((len(pieces) * units, part), dtype)
    return pl.pallas_call(
        turn_kernel,
        out_shape=(half, half),
        in_specs=[SMEM] + [HBM] * 4,
        out_specs=(VMEM, VMEM),
        scratch_shapes=[
            pltpu.VMEM((len(pieces), *pieces[0].shape), dtype),
            pltpu.SemaphoreType.DMA((len(pieces),)),
        ],
        compiler_params=roomy(58),
        cost_estimate=pl.CostEstimate(flops=COST, transcendentals=0, bytes_accessed=4 * 2**20),
    )(place, *pieces)


def split_kernel(which, down, down_kept, down_given):
    groups = down.shape[1] // (2 * SHARE)
    for side in range(2):

        @pl.when(which[0] == side)
        def _():
            for out, half in ((down_kept, side), (down_given, 1 - side)):
                firsts = [(2 * g + half) * SHARE for g in range(groups)]
                out[...] = jnp.concatenate([down[:, f : f + SHARE] for f in firsts], axis=1)


def split(which, down):
    width, hidden = down.shape
    half = jax.ShapeDtypeStruct((width, hidden // 2), down.dtype)
    return pl.pallas_call(
        split_kernel,
        out_shape=(half, half),
        in_specs=[SMEM, VMEM],
        out_specs=(VMEM, VMEM),
        compiler_params=roomy(16),
    )(which, down)


def product_kernel(weight, tokens, out):
    out[...] = dot(weight[...], tokens[...], 1, 1)


def product(weight, tokens):
    return pl.pallas_call(
        product_kernel,
        out_shape=jax.ShapeDtypeStruct((weight.shape[0], tokens.shape[0]), jnp.float32),
        in_specs=[VMEM] * 2,
        out_specs=VMEM,
        compiler_params=roomy(16),
    )(weight, tokens)


def product_onto_kernel(partial, weight, tokens, out):
    out[...] = (partial[...] + dot(weight[...], tokens[...], 1, 1)).astype(out.dtype)


def product_onto(partial, weight, tokens):
    return pl.pallas_call(
        product_onto_kernel,
        out_shape=jax.ShapeDtypeStruct(partial.shape, jnp.bfloat16),
        in_specs=[VMEM] * 3,
        out_specs=VMEM,
        compiler_params=roomy(16),
    )(partial, weight, tokens)


def down_far_kernel(weight, hidden, out):
    out[...] = dot(weight[...], hidden[...], 1, 0).astype(out.dtype)


def down_far_product(weight, hidden):
    return pl.pallas_call(
        down_far_kernel,
        out_shape=jax.ShapeDtypeStruct((weight.shape[0], hidden.shape[1]), jnp.bfloat16),
        in_specs=[VMEM] * 2,
        out_specs=VMEM,
        compiler_params=roomy(16),
    )(weight, hidden)


def down_sum_kernel(partial, arrived, out):
    total = partial[...] + arrived[...].astype(jnp.float32)
    out[...] = total.T.astype(out.dtype)


def down_sum(partial, arrived):
    return pl.pallas_call(
        down_sum_kernel,
        out_shape=jax.ShapeDtypeStruct(partial.shape[::-1], jnp.bfloat16),
        in_specs=[VMEM] * 2,
        out_specs=VMEM,
        compiler_params=roomy(16),
    )(partial, arrived)


def reorder_kernel(permutation, rows, out):
    out[...] = dot(permutation[...], rows[...], 1, 0).astype(out.dtype)


def reorder(permutation, rows):
    return pl.pallas_call(
        reorder_kernel,
        out_shape=jax.ShapeDtypeStruct(rows.shape, rows.dtype),
        in_specs=[VMEM] * 2,
        out_specs=VMEM,
        compiler_params=roomy(16),
    )(permutation, rows)


def combine_kernel(back, table, out):
    owners, rows, width = back.shape
    own = table.shape[0]
    groups = rows // own
    weight = jnp.concatenate([table[...]] * groups, axis=0)
    total = back[0].astype(jnp.float32) * weight[:, :1]
    for owner in range(1, owners):
        total = total + back[owner].astype(jnp.float32) * weight[:, owner : owner + 1]
    wide = jnp.concatenate([total[g * own : (g + 1) * own] for g in range(groups)], axis=1)
    out[...] = wide.astype(out.dtype)


def combine(back, table):
    owners, rows, width = back.shape
    own = table.shape[0]
    return pl.pallas_call(
        combine_kernel,
        out_shape=jax.ShapeDtypeStruct((own, rows // own * width), jnp.bfloat16),
        in_specs=[VMEM] * 2,
        out_specs=VMEM,
        compiler_params=roomy(16),
    )(back, table)


def per_device(tokens, expert_ids, scores, gate_weight, up_weight, down_weight):
    across = lax.axis_size(BLOCK)
    groups = lax.axis_size(GRP)
    owners = lax.axis_size("ex")
    side, col = lax.axis_index("side"), lax.axis_index(BLOCK)
    own, half_width = tokens.shape
    share = gate_weight.shape[2] // 2
    out_width = down_weight.shape[2]
    rows = own * owners
    total = rows * groups
    part = half_width // across

    lifted = jax.nn.sigmoid(scores)
    route_weight = 2.5 * lifted / jnp.sum(lifted, axis=-1, keepdims=True)
    named = expert_ids[:, :, None] == jnp.arange(owners, dtype=jnp.int32)
    table = jnp.sum(jnp.where(named, route_weight[:, :, None], 0.0), axis=1)
    def rows_of(step):
        start = (col ^ step) * part
        return jnp.stack(
            [lax.dynamic_slice_in_dim(w[0], start, part, 0) for w in (gate_weight, up_weight)]
        )

    pieces = [rows_of(0)] + [swap_in_block(rows_of(d), d) for d in range(1, across)]

    column = exchange(copies(tokens.reshape(-1, 4, 128), owners), "ex").reshape(rows, half_width)
    parts = jnp.transpose(column.reshape(rows, across, part), (1, 0, 2))
    which = side.reshape(1)
    down_kept, down_given = split(which, down_weight[0].T)
    down_far = lax.ppermute(down_given, "side", SWAP)
    parts, table, down_kept, down_far = lax.optimization_barrier(
        (parts, table, down_kept, down_far)
    )
    fan = jnp.broadcast_to(
        parts.reshape(1, 2, 1, 2, rows, part), (2, 2, 2, 2, rows, part)
    ).reshape(groups, rows, part)
    everyone = exchange(fan, GRP)
    kept, given = turn(jnp.stack([side, col]).astype(jnp.int32), pieces)
    given = lax.ppermute(given, "side", SWAP)
    everyone, kept, given = lax.optimization_barrier((everyone, kept, given))
    everyone = everyone.reshape(total, part)

    far = lax.ppermute(everyone, "side", SWAP)
    sums = product_onto(product(kept, everyone), given, far)
    sums = exchange(sums.reshape(across, 2 * share, total), BLOCK)
    summed = jnp.sum(sums.astype(jnp.float32), axis=0)
    hidden = (jax.nn.silu(summed[:share]) * summed[share:]).astype(jnp.bfloat16)

    mine = exchange(copies(hidden, groups), GRP).reshape(groups * share, total)
    outgoing = down_far_product(down_far, mine)
    outgoing, mine, index = lax.optimization_barrier(
        (outgoing, mine, jnp.arange(total, dtype=jnp.int32))
    )
    arrived = lax.ppermute(outgoing, "side", SWAP)
    source = (index // own) % groups * rows + index // (groups * own) * own + index % own
    permutation = (source[:, None] == index[None, :]).astype(jnp.bfloat16)
    partial = dot(down_kept, mine, 1, 0)
    partial, permutation, arrived = lax.optimization_barrier((partial, permutation, arrived))
    expert_out = down_sum(partial, arrived)

    by_group = exchange(expert_out.reshape(groups, rows, out_width), GRP).reshape(total, out_width)
    turned = reorder(permutation, by_group)
    turned, table = lax.optimization_barrier((turned, table))
    back = exchange(turned.reshape(owners, groups * own, out_width), "ex")
    return combine(back, table)


def solution(mesh):
    sides, groups, owners = mesh.devices.shape
    names = ("side", *GRP, "ex")
    fine = Mesh(mesh.devices.reshape(sides, 2, 2, 2, groups // 8, owners), names)
    in_specs = (
        P((*GRP, "ex"), "side"),
        P((*GRP, "ex"), None),
        P((*GRP, "ex"), None),
        P("ex", "side", GRP),
        P("ex", "side", GRP),
        P("ex", None, ("side", *GRP)),
    )
    out_specs = P((*GRP, "ex"), "side")
    return jax.shard_map(
        per_device, mesh=fine, in_specs=in_specs, out_specs=out_specs, check_vma=False
    )
```

```python
import jax
import jax.numpy as jnp
from jax import lax
from jax.experimental import pallas as pl
from jax.experimental.pallas import tpu as pltpu
from jax.sharding import Mesh
from jax.sharding import PartitionSpec as P

GRP = ("yh", "yl", "xh", "xl")
BLOCK = ("yl", "xl")
SWAP = [(0, 1), (1, 0)]
COST = 8 * 10**9
ALL = ("side", *GRP)


def dot(a, b, ca, cb):
    return lax.dot_general(
        a, b, (((ca,), (cb,)), ((), ())), preferred_element_type=jnp.float32
    )


def exchange(blocks, axis):
    return lax.all_to_all(blocks, axis, split_axis=0, concat_axis=0, tiled=True)


def copies(block, n):
    return jnp.broadcast_to(block[None], (n, *block.shape))


def swap_in_block(x, step):
    return lax.ppermute(x, BLOCK, [(i, i ^ step) for i in range(4)])


VMEM = pl.BlockSpec(memory_space=pltpu.VMEM)
SMEM = pl.BlockSpec(memory_space=pltpu.SMEM)
HBM = pl.BlockSpec(memory_space=pltpu.HBM)


def roomy(mib):
    return pltpu.CompilerParams(vmem_limit_bytes=mib * 2**20)


def pass_kernel(*refs):
    del refs


def pass_through(arrays):
    n = len(arrays)
    return pl.pallas_call(
        pass_kernel,
        out_shape=tuple(jax.ShapeDtypeStruct(a.shape, a.dtype) for a in arrays),
        in_specs=[HBM] * n,
        out_specs=(HBM,) * n,
        input_output_aliases={i: i for i in range(n)},
        compiler_params=roomy(58),
        cost_estimate=pl.CostEstimate(flops=COST, transcendentals=0, bytes_accessed=4 * 2**20),
    )(*arrays)


def gate_up_kernel(place, tokens, *refs):
    out, held, sems = refs[-3:]
    side, col = place[0], place[1]
    steps = out.shape[0]
    moves = [
        [
            pltpu.make_async_copy(
                refs[kind * steps + step], held.at[kind, step], sems.at[kind, step]
            )
            for kind in range(2)
        ]
        for step in range(steps)
    ]
    for pair in moves:
        for move in pair:
            move.start()
    for step in range(steps):
        total = None
        for kind in range(2):
            moves[step][kind].wait()
            weight = jnp.concatenate([held[kind, step, 0], held[kind, step, 1]], axis=1)
            some = dot(tokens[side if kind == 0 else 1 - side], weight, 1, 0)
            total = some if total is None else total + some
        out[col ^ step] = total.astype(out.dtype)


def gate_up(place, tokens, near, far):
    steps, units = len(near), near[0].shape[2]
    count = tokens.shape[1]
    return pl.pallas_call(
        gate_up_kernel,
        out_shape=jax.ShapeDtypeStruct((steps, count, 2 * units), tokens.dtype),
        in_specs=[SMEM, VMEM] + [HBM] * (2 * steps),
        out_specs=VMEM,
        scratch_shapes=[
            pltpu.VMEM((2, steps, *near[0].shape), tokens.dtype),
            pltpu.SemaphoreType.DMA((2, steps)),
        ],
        compiler_params=roomy(16),
    )(place, tokens, *near, *far)


def down_kernel(place, hidden, near, far, out):
    groups, _, units = hidden.shape
    for kind, weight in enumerate((near, far)):
        total = None
        for g in range(0, groups, 2):
            both = jnp.concatenate([hidden[g], hidden[g + 1]], axis=1)
            some = dot(both, weight[:, g * units : (g + 2) * units], 1, 1)
            total = some if total is None else total + some
        out[place[0] if kind == 0 else 1 - place[0]] = total.astype(out.dtype)


def down_product(place, hidden, near, far):
    return pl.pallas_call(
        down_kernel,
        out_shape=jax.ShapeDtypeStruct((2, hidden.shape[1], near.shape[0]), hidden.dtype),
        in_specs=[SMEM] + [VMEM] * 3,
        out_specs=VMEM,
        compiler_params=roomy(16),
    )(place, hidden, near, far)


def reorder_kernel(permutation, rows, out):
    out[...] = dot(permutation[...], rows[...], 1, 0).astype(out.dtype)


def reorder(permutation, rows):
    return pl.pallas_call(
        reorder_kernel,
        out_shape=jax.ShapeDtypeStruct(rows.shape, rows.dtype),
        in_specs=[VMEM] * 2,
        out_specs=VMEM,
        compiler_params=roomy(16),
    )(permutation, rows)


def combine_kernel(back, table, out):
    owners, rows, width = back.shape
    own = table.shape[0]
    groups = rows // own
    weight = jnp.concatenate([table[...]] * groups, axis=0)
    total = back[0].astype(jnp.float32) * weight[:, :1]
    for owner in range(1, owners):
        total = total + back[owner].astype(jnp.float32) * weight[:, owner : owner + 1]
    wide = jnp.concatenate([total[g * own : (g + 1) * own] for g in range(groups)], axis=1)
    out[...] = wide.astype(out.dtype)


def combine(back, table):
    owners, rows, width = back.shape
    own = table.shape[0]
    return pl.pallas_call(
        combine_kernel,
        out_shape=jax.ShapeDtypeStruct((own, rows // own * width), jnp.bfloat16),
        in_specs=[VMEM] * 2,
        out_specs=VMEM,
        compiler_params=roomy(16),
    )(back, table)


def per_device(tokens, expert_ids, scores, gate_weight, up_weight, down_weight):
    across = lax.axis_size(BLOCK)
    groups = lax.axis_size(GRP)
    owners = lax.axis_size("ex")
    side, col = lax.axis_index("side"), lax.axis_index(BLOCK)
    own, half_width = tokens.shape
    units = gate_weight.shape[2]
    out_width = down_weight.shape[2]
    rows = own * owners
    total = rows * groups
    part = half_width // across
    half = total // 2

    lifted = jax.nn.sigmoid(scores)
    route_weight = 2.5 * lifted / jnp.sum(lifted, axis=-1, keepdims=True)
    named = expert_ids[:, :, None] == jnp.arange(owners, dtype=jnp.int32)
    table = jnp.sum(jnp.where(named, route_weight[:, :, None], 0.0), axis=1)
    def rows_of(step):
        start = (col ^ step) * part
        return jnp.stack(
            [lax.dynamic_slice_in_dim(w[0], start, part, 0) for w in (gate_weight, up_weight)]
        )

    pieces = [rows_of(0)] + [swap_in_block(rows_of(d), d) for d in range(1, across)]

    column = exchange(copies(tokens.reshape(-1, 4, 128), owners), "ex").reshape(rows, half_width)
    parts = jnp.transpose(column.reshape(rows, across, part), (1, 0, 2))
    index = jnp.arange(total, dtype=jnp.int32)
    owner, group = index // (groups * own), index // own % groups
    source = owner // (owners // 2) * half + group * (rows // 2)
    source = source + owner % (owners // 2) * own + index % own
    permutation = (source[:, None] == index[None, :]).astype(jnp.bfloat16)
    parts, table, permutation = lax.optimization_barrier((parts, table, permutation))

    fan = jnp.transpose(parts.reshape(2, 2, 2, rows // 2, part), (2, 0, 1, 3, 4))
    fan = jnp.broadcast_to(fan[:, None, :, None], (2, 2, 2, 2, 2, rows // 2, part))
    everyone = exchange(fan.reshape(2 * groups, rows // 2, part), ALL)
    near = [pieces[0], *pass_through(pieces[1:])]
    far = [lax.ppermute(piece, "side", SWAP) for piece in near]
    down_near = down_weight[0].T
    down_far = lax.ppermute(down_near, "side", SWAP)
    everyone, near, far, down_far = lax.optimization_barrier((everyone, near, far, down_far))

    place = jnp.stack([side, col]).astype(jnp.int32)
    sums = exchange(gate_up(place, everyone.reshape(2, half, part), near, far), BLOCK)
    summed = jnp.sum(sums.astype(jnp.float32), axis=0)
    hidden = (jax.nn.silu(summed[:, :units]) * summed[:, units:]).astype(jnp.bfloat16)
    hidden = exchange(copies(hidden, groups), GRP)
    expert_out = down_product(place, hidden, down_near, down_far)

    by_group = exchange(expert_out.reshape(2 * groups, rows // 2, out_width), ALL)
    turned = reorder(permutation, by_group.reshape(total, out_width))
    back = exchange(turned.reshape(owners, groups * own, out_width), "ex")
    return combine(back, table)


def solution(mesh):
    sides, groups, owners = mesh.devices.shape
    names = ("side", *GRP, "ex")
    fine = Mesh(mesh.devices.reshape(sides, 2, 2, 2, groups // 8, owners), names)
    in_specs = (
        P((*GRP, "ex"), "side"),
        P((*GRP, "ex"), None),
        P((*GRP, "ex"), None),
        P("ex", "side", GRP),
        P("ex", "side", GRP),
        P("ex", None, ("side", *GRP)),
    )
    out_specs = P((*GRP, "ex"), "side")
    return jax.shard_map(
        per_device, mesh=fine, in_specs=in_specs, out_specs=out_specs, check_vma=False
    )
```

```python
import jax
import jax.numpy as jnp
from jax import lax
from jax.experimental import pallas as pl
from jax.experimental.pallas import tpu as pltpu
from jax.sharding import Mesh
from jax.sharding import PartitionSpec as P

GRP = ("yh", "yl", "xh", "xl")
BLOCK = ("yl", "xl")
SWAP = [(0, 1), (1, 0)]
COST = 8 * 10**9
ALL = ("side", *GRP)


def dot(a, b, ca, cb):
    return lax.dot_general(
        a, b, (((ca,), (cb,)), ((), ())), preferred_element_type=jnp.float32
    )


def exchange(blocks, axis):
    return lax.all_to_all(blocks, axis, split_axis=0, concat_axis=0, tiled=True)


def copies(block, n):
    return jnp.broadcast_to(block[None], (n, *block.shape))


def swap_in_block(x, step):
    return lax.ppermute(x, BLOCK, [(i, i ^ step) for i in range(4)])


VMEM = pl.BlockSpec(memory_space=pltpu.VMEM)
SMEM = pl.BlockSpec(memory_space=pltpu.SMEM)
HBM = pl.BlockSpec(memory_space=pltpu.HBM)


def roomy(mib):
    return pltpu.CompilerParams(vmem_limit_bytes=mib * 2**20)


def pass_kernel(*refs):
    del refs


def pass_through(arrays):
    n = len(arrays)
    return pl.pallas_call(
        pass_kernel,
        out_shape=tuple(jax.ShapeDtypeStruct(a.shape, a.dtype) for a in arrays),
        in_specs=[HBM] * n,
        out_specs=(HBM,) * n,
        input_output_aliases={i: i for i in range(n)},
        compiler_params=roomy(58),
        cost_estimate=pl.CostEstimate(flops=COST, transcendentals=0, bytes_accessed=4 * 2**20),
    )(*arrays)


def gate_up_kernel(place, tokens, *refs):
    out, held, sems = refs[-3:]
    side, col = place[0], place[1]
    steps = out.shape[0]
    moves = [
        [
            pltpu.make_async_copy(
                refs[kind * steps + step], held.at[kind, step], sems.at[kind, step]
            )
            for kind in range(2)
        ]
        for step in range(steps)
    ]
    for kind in range(2):
        for step in range(steps):
            moves[step][kind].start()
    total = None
    for kind in range(2):
        for step in range(steps):
            moves[step][kind].wait()
        weight = jnp.concatenate(
            [held[kind, step, which] for step in range(steps) for which in range(2)], axis=1
        )
        some = dot(tokens[side if kind == 0 else 1 - side], weight, 1, 0)
        total = some if total is None else total + some
    width = out.shape[2]
    for step in range(steps):
        out[col ^ step] = total[:, step * width : (step + 1) * width].astype(out.dtype)


def gate_up(place, tokens, near, far):
    steps, units = len(near), near[0].shape[2]
    count = tokens.shape[1]
    return pl.pallas_call(
        gate_up_kernel,
        out_shape=jax.ShapeDtypeStruct((steps, count, 2 * units), tokens.dtype),
        in_specs=[SMEM, VMEM] + [HBM] * (2 * steps),
        out_specs=VMEM,
        scratch_shapes=[
            pltpu.VMEM((2, steps, *near[0].shape), tokens.dtype),
            pltpu.SemaphoreType.DMA((2, steps)),
        ],
        compiler_params=roomy(16),
    )(place, tokens, *near, *far)


def down_kernel(place, hidden, near, far, out):
    wide = jnp.concatenate([hidden[g] for g in range(hidden.shape[0])], axis=1)
    for kind, weight in enumerate((near, far)):
        total = dot(wide, weight[...], 1, 1)
        out[place[0] if kind == 0 else 1 - place[0]] = total.astype(out.dtype)


def down_product(place, hidden, near, far):
    return pl.pallas_call(
        down_kernel,
        out_shape=jax.ShapeDtypeStruct((2, hidden.shape[1], near.shape[0]), hidden.dtype),
        in_specs=[SMEM] + [VMEM] * 3,
        out_specs=VMEM,
        compiler_params=roomy(16),
    )(place, hidden, near, far)


def reorder_kernel(permutation, rows, out):
    out[...] = dot(permutation[...], rows[...], 1, 0).astype(out.dtype)


def reorder(permutation, rows):
    return pl.pallas_call(
        reorder_kernel,
        out_shape=jax.ShapeDtypeStruct(rows.shape, rows.dtype),
        in_specs=[VMEM] * 2,
        out_specs=VMEM,
        compiler_params=roomy(16),
    )(permutation, rows)


def combine_kernel(back, table, out):
    owners, rows, width = back.shape
    own = table.shape[0]
    groups = rows // own
    weight = jnp.concatenate([table[...]] * groups, axis=0)
    total = back[0].astype(jnp.float32) * weight[:, :1]
    for owner in range(1, owners):
        total = total + back[owner].astype(jnp.float32) * weight[:, owner : owner + 1]
    wide = jnp.concatenate([total[g * own : (g + 1) * own] for g in range(groups)], axis=1)
    out[...] = wide.astype(out.dtype)


def combine(back, table):
    owners, rows, width = back.shape
    own = table.shape[0]
    return pl.pallas_call(
        combine_kernel,
        out_shape=jax.ShapeDtypeStruct((own, rows // own * width), jnp.bfloat16),
        in_specs=[VMEM] * 2,
        out_specs=VMEM,
        compiler_params=roomy(16),
    )(back, table)


def per_device(tokens, expert_ids, scores, gate_weight, up_weight, down_weight):
    across = lax.axis_size(BLOCK)
    groups = lax.axis_size(GRP)
    owners = lax.axis_size("ex")
    side, col = lax.axis_index("side"), lax.axis_index(BLOCK)
    own, half_width = tokens.shape
    units = gate_weight.shape[2]
    out_width = down_weight.shape[2]
    rows = own * owners
    total = rows * groups
    part = half_width // across
    half = total // 2

    lifted = jax.nn.sigmoid(scores)
    route_weight = 2.5 * lifted / jnp.sum(lifted, axis=-1, keepdims=True)
    named = expert_ids[:, :, None] == jnp.arange(owners, dtype=jnp.int32)
    table = jnp.sum(jnp.where(named, route_weight[:, :, None], 0.0), axis=1)
    def rows_of(step):
        start = (col ^ step) * part
        return jnp.stack(
            [lax.dynamic_slice_in_dim(w[0], start, part, 0) for w in (gate_weight, up_weight)]
        )

    pieces = [rows_of(0)] + [swap_in_block(rows_of(d), d) for d in range(1, across)]

    column = exchange(copies(tokens.reshape(-1, 4, 128), owners), "ex").reshape(rows, half_width)
    parts = jnp.transpose(column.reshape(rows, across, part), (1, 0, 2))
    parts, table = lax.optimization_barrier((parts, table))

    fan = jnp.transpose(parts.reshape(2, 2, 2, rows // 2, part), (2, 0, 1, 3, 4))
    fan = jnp.broadcast_to(fan[:, None, :, None], (2, 2, 2, 2, 2, rows // 2, part))
    everyone = exchange(fan.reshape(2 * groups, rows // 2, part), ALL)
    near = [pieces[0], *pass_through(pieces[1:])]
    far = [lax.ppermute(piece, "side", SWAP) for piece in near]
    down_near = down_weight[0].T
    down_far = lax.ppermute(down_near, "side", SWAP)
    everyone, near, far, down_far, index = lax.optimization_barrier(
        (everyone, near, far, down_far, jnp.arange(total, dtype=jnp.int32))
    )

    place = jnp.stack([side, col]).astype(jnp.int32)
    sums = exchange(gate_up(place, everyone.reshape(2, half, part), near, far), BLOCK)
    summed = jnp.sum(sums.astype(jnp.float32), axis=0)
    hidden = (jax.nn.silu(summed[:, :units]) * summed[:, units:]).astype(jnp.bfloat16)
    hidden = exchange(copies(hidden, groups), GRP)
    expert_out = down_product(place, hidden, down_near, down_far)

    owner, group = index // (groups * own), index // own % groups
    source = owner // (owners // 2) * half + group * (rows // 2)
    source = source + owner % (owners // 2) * own + index % own
    permutation = (source[:, None] == index[None, :]).astype(jnp.bfloat16)
    expert_out, permutation = lax.optimization_barrier((expert_out, permutation))
    by_group = exchange(expert_out.reshape(2 * groups, rows // 2, out_width), ALL)
    turned = reorder(permutation, by_group.reshape(total, out_width))
    back = exchange(turned.reshape(owners, groups * own, out_width), "ex")
    return combine(back, table)


def solution(mesh):
    sides, groups, owners = mesh.devices.shape
    names = ("side", *GRP, "ex")
    fine = Mesh(mesh.devices.reshape(sides, 2, 2, 2, groups // 8, owners), names)
    in_specs = (
        P((*GRP, "ex"), "side"),
        P((*GRP, "ex"), None),
        P((*GRP, "ex"), None),
        P("ex", "side", GRP),
        P("ex", "side", GRP),
        P("ex", None, ("side", *GRP)),
    )
    out_specs = P((*GRP, "ex"), "side")
    return jax.shard_map(
        per_device, mesh=fine, in_specs=in_specs, out_specs=out_specs, check_vma=False
    )
```

```python
import functools

import jax
import jax.numpy as jnp
from jax import lax
from jax.experimental import pallas as pl
from jax.experimental.pallas import tpu as pltpu
from jax.sharding import Mesh
from jax.sharding import PartitionSpec as P

GRP = ("yh", "yl", "xh", "xl")
BLOCK = ("yl", "xl")
SWAP = [(0, 1), (1, 0)]
COST = 8 * 10**9
ALL = ("side", *GRP)


def dot(a, b, ca, cb):
    return lax.dot_general(
        a, b, (((ca,), (cb,)), ((), ())), preferred_element_type=jnp.float32
    )


def exchange(blocks, axis):
    return lax.all_to_all(blocks, axis, split_axis=0, concat_axis=0, tiled=True)


def copies(block, n):
    return jnp.broadcast_to(block[None], (n, *block.shape))


def swap_in_block(x, step):
    return lax.ppermute(x, BLOCK, [(i, i ^ step) for i in range(4)])


VMEM = pl.BlockSpec(memory_space=pltpu.VMEM)
SMEM = pl.BlockSpec(memory_space=pltpu.SMEM)
HBM = pl.BlockSpec(memory_space=pltpu.HBM)


def roomy(mib):
    return pltpu.CompilerParams(vmem_limit_bytes=mib * 2**20)


def pass_kernel(*refs):
    del refs


def pass_through(arrays):
    n = len(arrays)
    return pl.pallas_call(
        pass_kernel,
        out_shape=tuple(jax.ShapeDtypeStruct(a.shape, a.dtype) for a in arrays),
        in_specs=[HBM] * n,
        out_specs=(HBM,) * n,
        input_output_aliases={i: i for i in range(n)},
        compiler_params=roomy(58),
        cost_estimate=pl.CostEstimate(flops=COST, transcendentals=0, bytes_accessed=4 * 2**20),
    )(*arrays)


def gate_up_kernel(last, place, tokens, *refs):
    out, held, sems = refs[-3:]
    steps = held.shape[0]
    moves = [
        pltpu.make_async_copy(refs[step], held.at[step], sems.at[step]) for step in range(steps)
    ]
    for move in moves:
        move.start()
    for move in moves:
        move.wait()
    weight = jnp.concatenate(
        [held[step, which] for step in range(steps) for which in range(2)], axis=1
    )
    total = dot(tokens[...], weight, 1, 0)
    if not last:
        out[...] = total
        return
    total = total + refs[steps][...]
    width = out.shape[2]
    for step in range(steps):
        block = total[:, step * width : (step + 1) * width]
        out[place[0] ^ step] = block.astype(out.dtype)


def gate_up(place, tokens, pieces, partial=None):
    steps, units = len(pieces), pieces[0].shape[2]
    count = tokens.shape[0]
    last = partial is not None
    shape = (steps, count, 2 * units) if last else (count, steps * 2 * units)
    return pl.pallas_call(
        functools.partial(gate_up_kernel, last),
        out_shape=jax.ShapeDtypeStruct(shape, tokens.dtype if last else jnp.float32),
        in_specs=[SMEM, VMEM] + [HBM] * steps + [VMEM] * last,
        out_specs=VMEM,
        scratch_shapes=[
            pltpu.VMEM((steps, *pieces[0].shape), tokens.dtype),
            pltpu.SemaphoreType.DMA((steps,)),
        ],
        compiler_params=roomy(16),
    )(place, tokens, *pieces, *([partial] if last else []))


def down_kernel(place, hidden, near, far, out):
    wide = jnp.concatenate([hidden[g] for g in range(hidden.shape[0])], axis=1)
    for kind, weight in enumerate((near, far)):
        total = dot(wide, weight[...], 1, 1)
        out[place[0] if kind == 0 else 1 - place[0]] = total.astype(out.dtype)


def down_product(place, hidden, near, far):
    return pl.pallas_call(
        down_kernel,
        out_shape=jax.ShapeDtypeStruct((2, hidden.shape[1], near.shape[0]), hidden.dtype),
        in_specs=[SMEM] + [VMEM] * 3,
        out_specs=VMEM,
        compiler_params=roomy(16),
    )(place, hidden, near, far)


def reorder_kernel(permutation, rows, out):
    out[...] = dot(permutation[...], rows[...], 1, 0).astype(out.dtype)


def reorder(permutation, rows):
    return pl.pallas_call(
        reorder_kernel,
        out_shape=jax.ShapeDtypeStruct(rows.shape, rows.dtype),
        in_specs=[VMEM] * 2,
        out_specs=VMEM,
        compiler_params=roomy(16),
    )(permutation, rows)


def combine_kernel(back, table, out):
    owners, rows, width = back.shape
    own = table.shape[0]
    groups = rows // own
    weight = jnp.concatenate([table[...]] * groups, axis=0)
    total = back[0].astype(jnp.float32) * weight[:, :1]
    for owner in range(1, owners):
        total = total + back[owner].astype(jnp.float32) * weight[:, owner : owner + 1]
    wide = jnp.concatenate([total[g * own : (g + 1) * own] for g in range(groups)], axis=1)
    out[...] = wide.astype(out.dtype)


def combine(back, table):
    owners, rows, width = back.shape
    own = table.shape[0]
    return pl.pallas_call(
        combine_kernel,
        out_shape=jax.ShapeDtypeStruct((own, rows // own * width), jnp.bfloat16),
        in_specs=[VMEM] * 2,
        out_specs=VMEM,
        compiler_params=roomy(16),
    )(back, table)


def per_device(tokens, expert_ids, scores, gate_weight, up_weight, down_weight):
    across = lax.axis_size(BLOCK)
    groups = lax.axis_size(GRP)
    owners = lax.axis_size("ex")
    side, col = lax.axis_index("side"), lax.axis_index(BLOCK)
    own, half_width = tokens.shape
    units = gate_weight.shape[2]
    out_width = down_weight.shape[2]
    rows = own * owners
    total = rows * groups
    part = half_width // across
    half = total // 2

    lifted = jax.nn.sigmoid(scores)
    route_weight = 2.5 * lifted / jnp.sum(lifted, axis=-1, keepdims=True)
    named = expert_ids[:, :, None] == jnp.arange(owners, dtype=jnp.int32)
    table = jnp.sum(jnp.where(named, route_weight[:, :, None], 0.0), axis=1)
    def rows_of(step):
        start = (col ^ step) * part
        return jnp.stack(
            [lax.dynamic_slice_in_dim(w[0], start, part, 0) for w in (gate_weight, up_weight)]
        )

    pieces = [rows_of(0)] + [swap_in_block(rows_of(d), d) for d in range(1, across)]

    column = exchange(copies(tokens.reshape(-1, 4, 128), owners), "ex").reshape(rows, half_width)
    parts = jnp.transpose(column.reshape(rows, across, part), (1, 0, 2))
    parts, table, down_near = lax.optimization_barrier((parts, table, down_weight[0].T))

    fan = jnp.broadcast_to(
        parts.reshape(1, 2, 1, 2, rows, part), (2, 2, 2, 2, rows, part)
    ).reshape(groups, rows, part)
    everyone = exchange(fan, GRP)
    near = [pieces[0], *pass_through(pieces[1:])]
    far = [lax.ppermute(piece, "side", SWAP) for piece in near]
    down_far = lax.ppermute(down_near, "side", SWAP)
    everyone, near, far, down_far, index = lax.optimization_barrier(
        (everyone, near, far, down_far, jnp.arange(total, dtype=jnp.int32))
    )

    def half_of(which):
        some = lax.dynamic_slice_in_dim(everyone, which * (rows // 2), rows // 2, 1)
        return some.reshape(half, part)

    arrived = lax.ppermute(half_of(1 - side), "side", SWAP)
    partial = gate_up(col.reshape(1), half_of(side), near)
    owner, group = index // (groups * own), index // own % groups
    source = owner // (owners // 2) * half + group * (rows // 2)
    source = source + owner % (owners // 2) * own + index % own
    permutation = (source[:, None] == index[None, :]).astype(jnp.bfloat16)
    sums = gate_up(col.reshape(1), arrived, far, partial)
    sums, permutation = lax.optimization_barrier((sums, permutation))
    sums = exchange(sums, BLOCK)
    summed = jnp.sum(sums.astype(jnp.float32), axis=0)
    hidden = (jax.nn.silu(summed[:, :units]) * summed[:, units:]).astype(jnp.bfloat16)
    hidden = exchange(copies(hidden, groups), GRP)
    expert_out = down_product(side.reshape(1), hidden, down_near, down_far)

    by_group = exchange(expert_out.reshape(2 * groups, rows // 2, out_width), ALL)
    turned = reorder(permutation, by_group.reshape(total, out_width))
    back = exchange(turned.reshape(owners, groups * own, out_width), "ex")
    return combine(back, table)


def solution(mesh):
    sides, groups, owners = mesh.devices.shape
    names = ("side", *GRP, "ex")
    fine = Mesh(mesh.devices.reshape(sides, 2, 2, 2, groups // 8, owners), names)
    in_specs = (
        P((*GRP, "ex"), "side"),
        P((*GRP, "ex"), None),
        P((*GRP, "ex"), None),
        P("ex", "side", GRP),
        P("ex", "side", GRP),
        P("ex", None, ("side", *GRP)),
    )
    out_specs = P((*GRP, "ex"), "side")
    return jax.shard_map(
        per_device, mesh=fine, in_specs=in_specs, out_specs=out_specs, check_vma=False
    )
```

```python
import jax
import jax.numpy as jnp
from jax import lax
from jax.experimental import pallas as pl
from jax.experimental.pallas import tpu as pltpu
from jax.sharding import Mesh
from jax.sharding import PartitionSpec as P

GRP = ("yh", "yl", "xh", "xl")
BLOCK = ("yl", "xl")
SWAP = [(0, 1), (1, 0)]
COST = 30 * 10**9
SHARE = 64


def dot(a, b, ca, cb):
    return lax.dot_general(
        a, b, (((ca,), (cb,)), ((), ())), preferred_element_type=jnp.float32
    )


def exchange(blocks, axis):
    return lax.all_to_all(blocks, axis, split_axis=0, concat_axis=0, tiled=True)


def copies(block, n):
    return jnp.broadcast_to(block[None], (n, *block.shape))


def swap_in_block(x, step):
    return lax.ppermute(x, BLOCK, [(i, i ^ step) for i in range(4)])


VMEM = pl.BlockSpec(memory_space=pltpu.VMEM)
SMEM = pl.BlockSpec(memory_space=pltpu.SMEM)
HBM = pl.BlockSpec(memory_space=pltpu.HBM)


def roomy(mib):
    return pltpu.CompilerParams(vmem_limit_bytes=mib * 2**20)


def turn_kernel(place, piece0, piece1, piece2, piece3, kept, given, held, sems):
    pieces = (piece0, piece1, piece2, piece3)
    units = held.shape[3]
    share = units // 2
    moves = [
        pltpu.make_async_copy(piece, held.at[step], sems.at[step])
        for step, piece in enumerate(pieces)
    ]
    for move in moves:
        move.start()
    for step, move in enumerate(moves):
        move.wait()
        first = pl.multiple_of((place[1] ^ step) * units, units)
        for side in range(2):

            @pl.when(place[0] == side)
            def _():
                for kind in range(2):
                    turned = held[step, kind].T
                    near, far = side * share, (1 - side) * share
                    rows = pl.ds(pl.multiple_of(first + kind * share, share), share)
                    kept[rows, :] = turned[near : near + share]
                    given[rows, :] = turned[far : far + share]


def turn(place, pieces):
    part, units = pieces[0].shape[1:]
    dtype = pieces[0].dtype
    half = jax.ShapeDtypeStruct((len(pieces) * units, part), dtype)
    return pl.pallas_call(
        turn_kernel,
        out_shape=(half, half),
        in_specs=[SMEM] + [HBM] * 4,
        out_specs=(VMEM, VMEM),
        scratch_shapes=[
            pltpu.VMEM((len(pieces), *pieces[0].shape), dtype),
            pltpu.SemaphoreType.DMA((len(pieces),)),
        ],
        compiler_params=roomy(58),
        cost_estimate=pl.CostEstimate(flops=COST, transcendentals=0, bytes_accessed=4 * 2**20),
    )(place, *pieces)


def split_kernel(which, down, down_kept, down_given):
    groups = down.shape[1] // (2 * SHARE)
    for side in range(2):

        @pl.when(which[0] == side)
        def _():
            for out, half in ((down_kept, side), (down_given, 1 - side)):
                firsts = [(2 * g + half) * SHARE for g in range(groups)]
                out[...] = jnp.concatenate([down[:, f : f + SHARE] for f in firsts], axis=1)


def split(which, down):
    width, hidden = down.shape
    half = jax.ShapeDtypeStruct((width, hidden // 2), down.dtype)
    return pl.pallas_call(
        split_kernel,
        out_shape=(half, half),
        in_specs=[SMEM, VMEM],
        out_specs=(VMEM, VMEM),
        compiler_params=roomy(16),
    )(which, down)


def product_kernel(weight, tokens, out):
    out[...] = dot(weight[...], tokens[...], 1, 1)


def product(weight, tokens):
    return pl.pallas_call(
        product_kernel,
        out_shape=jax.ShapeDtypeStruct((weight.shape[0], tokens.shape[0]), jnp.float32),
        in_specs=[VMEM] * 2,
        out_specs=VMEM,
        compiler_params=roomy(16),
    )(weight, tokens)


def product_onto_kernel(partial, weight, tokens, out):
    out[...] = (partial[...] + dot(weight[...], tokens[...], 1, 1)).astype(out.dtype)


def product_onto(partial, weight, tokens):
    return pl.pallas_call(
        product_onto_kernel,
        out_shape=jax.ShapeDtypeStruct(partial.shape, jnp.bfloat16),
        in_specs=[VMEM] * 3,
        out_specs=VMEM,
        compiler_params=roomy(16),
    )(partial, weight, tokens)


def down_kernel(partial, weight, hidden, out):
    total = partial[...] + dot(weight[...], hidden[...], 1, 0)
    out[...] = total.T.astype(out.dtype)


def down_product(partial, weight, hidden):
    return pl.pallas_call(
        down_kernel,
        out_shape=jax.ShapeDtypeStruct(partial.shape[::-1], jnp.bfloat16),
        in_specs=[VMEM] * 3,
        out_specs=VMEM,
        compiler_params=roomy(16),
    )(partial, weight, hidden)


def reorder_kernel(permutation, rows, out):
    total = dot(permutation[...], rows[...], 1, 0)
    count = total.shape[0] // out.shape[0]
    for owner in range(out.shape[0]):
        block = total[owner * count : (owner + 1) * count]
        tail = block[:, 128:]
        last = [tail[40:48, 32 * k : 32 * (k + 1)] for k in range(3)]
        last = jnp.concatenate(last + [jnp.zeros((16, 32), jnp.float32)], axis=0)
        low = jnp.concatenate([tail[:40], last], axis=1)
        out[owner] = jnp.concatenate([block[:, :128], low], axis=0).astype(out.dtype)


def reorder(permutation, rows, owners):
    return pl.pallas_call(
        reorder_kernel,
        out_shape=jax.ShapeDtypeStruct((owners, 88, 128), rows.dtype),
        in_specs=[VMEM] * 2,
        out_specs=VMEM,
        compiler_params=roomy(16),
    )(permutation, rows)


def combine_kernel(back, table, out):
    owners = back.shape[0]
    own = table.shape[0]
    groups = 48 // own
    weight = jnp.concatenate([table[...]] * groups, axis=0)
    spread = jnp.concatenate([weight[40:48]] * 5, axis=0)
    lane = lax.broadcasted_iota(jnp.int32, (40, 128), 1)
    total = None
    for owner in range(owners):
        at = slice(owner, owner + 1)
        high = jnp.broadcast_to(weight[:, at], (48, 128))
        low = jnp.where(lane < 96, weight[:40, at], spread[:, at])
        some = back[owner].astype(jnp.float32) * jnp.concatenate([high, low], axis=0)
        total = some if total is None else total + some
    low = total[48:]
    last = jnp.concatenate([low[8 * k : 8 * (k + 1), 96:] for k in range(3)], axis=1)
    tail = jnp.concatenate([low[:, :96], last], axis=0)
    total = jnp.concatenate([total[:48], tail], axis=1)
    wide = jnp.concatenate([total[g * own : (g + 1) * own] for g in range(groups)], axis=1)
    out[...] = wide.astype(out.dtype)


def combine(back, table):
    own = table.shape[0]
    return pl.pallas_call(
        combine_kernel,
        out_shape=jax.ShapeDtypeStruct((own, 48 // own * 224), jnp.bfloat16),
        in_specs=[VMEM] * 2,
        out_specs=VMEM,
        compiler_params=roomy(16),
    )(back, table)


def per_device(tokens, expert_ids, scores, gate_weight, up_weight, down_weight):
    across = lax.axis_size(BLOCK)
    groups = lax.axis_size(GRP)
    owners = lax.axis_size("ex")
    side, col = lax.axis_index("side"), lax.axis_index(BLOCK)
    own, half_width = tokens.shape
    share = gate_weight.shape[2] // 2
    out_width = down_weight.shape[2]
    rows = own * owners
    total = rows * groups
    part = half_width // across

    lifted = jax.nn.sigmoid(scores)
    route_weight = 2.5 * lifted / jnp.sum(lifted, axis=-1, keepdims=True)
    named = expert_ids[:, :, None] == jnp.arange(owners, dtype=jnp.int32)
    table = jnp.sum(jnp.where(named, route_weight[:, :, None], 0.0), axis=1)
    def rows_of(step):
        start = (col ^ step) * part
        return jnp.stack(
            [lax.dynamic_slice_in_dim(w[0], start, part, 0) for w in (gate_weight, up_weight)]
        )

    pieces = [rows_of(0)] + [swap_in_block(rows_of(d), d) for d in range(1, across)]

    column = exchange(copies(tokens.reshape(-1, 4, 128), owners), "ex").reshape(rows, half_width)
    parts = jnp.transpose(column.reshape(rows, across, part), (1, 0, 2))
    parts, table = lax.optimization_barrier((parts, table))
    fan = jnp.broadcast_to(
        parts.reshape(1, 2, 1, 2, rows, part), (2, 2, 2, 2, rows, part)
    ).reshape(groups, rows, part)
    everyone = exchange(fan, GRP)
    which = side.reshape(1)
    kept, given = turn(jnp.stack([side, col]).astype(jnp.int32), pieces)
    given = lax.ppermute(given, "side", SWAP)
    everyone, kept, given = lax.optimization_barrier((everyone, kept, given))
    everyone = everyone.reshape(total, part)

    far = lax.ppermute(everyone, "side", SWAP)
    sums = product_onto(product(kept, everyone), given, far)
    sums = exchange(sums.reshape(across, 2 * share, total), BLOCK)
    summed = jnp.sum(sums.astype(jnp.float32), axis=0)
    hidden = (jax.nn.silu(summed[:share]) * summed[share:]).astype(jnp.bfloat16)

    mine = exchange(copies(hidden, groups), GRP).reshape(groups * share, total)
    mine, which, index = lax.optimization_barrier(
        (mine, which, jnp.arange(total, dtype=jnp.int32))
    )
    other = lax.ppermute(mine, "side", SWAP)
    down_kept, down_given = split(which, down_weight[0].T)
    source = (index // own) % groups * rows + index // (groups * own) * own + index % own
    permutation = (source[:, None] == index[None, :]).astype(jnp.bfloat16)
    partial = dot(down_kept, mine, 1, 0)
    partial, permutation, other = lax.optimization_barrier((partial, permutation, other))
    expert_out = down_product(partial, down_given, other)

    by_group = exchange(expert_out.reshape(groups, rows, out_width), GRP).reshape(total, out_width)
    turned = reorder(permutation, by_group, owners)
    turned, table = lax.optimization_barrier((turned, table))
    back = exchange(turned, "ex")
    return combine(back, table)


def solution(mesh):
    sides, groups, owners = mesh.devices.shape
    names = ("side", *GRP, "ex")
    fine = Mesh(mesh.devices.reshape(sides, 2, 2, 2, groups // 8, owners), names)
    in_specs = (
        P((*GRP, "ex"), "side"),
        P((*GRP, "ex"), None),
        P((*GRP, "ex"), None),
        P("ex", "side", GRP),
        P("ex", "side", GRP),
        P("ex", None, ("side", *GRP)),
    )
    out_specs = P((*GRP, "ex"), "side")
    return jax.shard_map(
        per_device, mesh=fine, in_specs=in_specs, out_specs=out_specs, check_vma=False
    )
```
